512 devices in a mesh: rep: 32 (over z, y_hi), sp: 16 (over y_lo, x, core).
Axes of the slice: x: 4, y: 8 (y_hi: 4, y_lo: 2; y = y_hi * 2 + y_lo), z: 8, core: 2. Of those that a mesh axis runs over, the one named last changes fastest.
Arguments:
- queries: bfloat16 [32, 3072, 2048], P('rep', 'sp'), may hold values from -13 to 13
- key_rows: bfloat16 [32, 3072, 2048], P('rep', 'sp'), may hold values from -13 to 13
- values: bfloat16 [32, 3072, 2048], P('rep', 'sp'), may hold values from -6 to 6
- out_grad: bfloat16 [32, 3072, 3072], P('rep', 'sp'), may hold values from -6 to 6
- clip_count: int32 [32], P('rep'), may hold values from 1 to 3, as said below
- clip_lengths: int32 [32, 3], P('rep'), may hold values from 0 to 3072, as said below
- adapter_in: float32 [2048, 128], P('sp'), may hold values from -4 to 4
- adapter_out: float32 [128, 3072], P('sp'), may hold values from -4 to 4
- moment_in: float32 [2048, 128], P('sp'), may hold values from -3 to 3
- square_in: float32 [2048, 128], P('sp'), may hold values from 0.05 to 2
- moment_out: float32 [128, 3072], P('sp'), may hold values from -3 to 3
- square_out: float32 [128, 3072], P('sp'), may hold values from 0.05 to 2
Outputs:
- momentum_in: float32 [2048, 128], P('sp')
- variance_in: float32 [2048, 128], P('sp')
- update_in: float32 [2048, 128], P('sp')
- momentum_out: float32 [128, 3072], P('sp')
- variance_out: float32 [128, 3072], P('sp')
- update_out: float32 [128, 3072], P('sp')
The draws below stay inside these ranges and needn't reach their ends.
Inputs may be any that keep to these rules, and one draw needn't show every extreme that they name: `clip_count`: in every draw some replica has 1 clip and some replica has 3. `clip_lengths`: each entry is a multiple of 384; entries at or beyond a replica's clip count are 0, the others 384 or more; the entries of a replica sum to at most 3072, and in every draw some replica holds a single clip of exactly 3072.
All inputs are finite; a program needn't handle non-finite values.
Results may differ from the reference program's by a relative error of at most 0.0017.
Values may be sent and summed in bfloat16 or wider, within the bound.
A program may use at most 64 MiB of HBM per device.

```python
import math
import jax
import jax.numpy as jnp
from jax import lax

D = 3072
HD = 128
RANK = 128
HEADS = 16
INNER = 2048
TOKENS = 3072
UNIT = 384
REPS = 32


def clip_layout(key):
    base = jax.random.fold_in(key, 101)
    streams = jax.random.split(base, 5)
    fullest = jax.random.randint(streams[1], (), 0, REPS)
    index = jnp.arange(REPS)
    drawn = jax.random.randint(streams[0], (REPS,), 1, 4)
    counts = jnp.where(index == fullest, 1, jnp.where(index == (fullest + 1) % REPS, 3, drawn))
    spread = jax.random.randint(streams[2], (REPS,), counts, 9)
    units = jnp.where(index == fullest, 8, spread)
    first_draw = jax.random.randint(streams[3], (REPS,), 1, units - counts + 2)
    first_units = jnp.where(counts == 1, units, first_draw)
    remain = units - first_units
    second_draw = jax.random.randint(streams[4], (REPS,), 1, jnp.maximum(remain - 1, 1) + 1)
    second_units = jnp.where(counts == 1, 0, jnp.where(counts == 2, remain, second_draw))
    third_units = jnp.where(counts == 3, remain - second_units, 0)
    lengths = jnp.stack([first_units, second_units, third_units], axis=1) * UNIT
    return (counts.astype(jnp.int32), lengths.astype(jnp.int32))


def drawn_pairs(key):
    base = jax.random.fold_in(key, 202)
    streams = jax.random.split(base, 2)
    shape = (REPS, TOKENS, INNER)
    queries = jax.random.truncated_normal(streams[0], -4.0, 4.0, shape, jnp.float32)
    key_rows = jax.random.truncated_normal(streams[1], -4.0, 4.0, shape, jnp.float32)
    return (queries, key_rows)


def draw_queries(key, part):
    return drawn_pairs(key)[0].astype(jnp.bfloat16)


def draw_key_rows(key, part):
    return drawn_pairs(key)[1].astype(jnp.bfloat16)


def draw_clip_count(key, part):
    return clip_layout(key)[0]


def draw_clip_lengths(key, part):
    return clip_layout(key)[1]


def shard_levels(stream_key, shape, cuts, low, top_value):
    loudness = 1.0
    for dim, blocks in cuts:
        draws = jax.random.uniform(jax.random.fold_in(jax.random.fold_in(stream_key, 6), dim), (blocks,), jnp.float32, low / len(cuts), top_value / len(cuts))
        loudness = loudness * jnp.repeat(jnp.exp(draws), shape[dim] // blocks).reshape((-1,) + (1,) * (len(shape) - 1 - dim))
    return loudness


def scatter_about(own_key, dims, width, bound, pieces=(), held_as=jnp.bfloat16):
    values = width * jax.random.normal(own_key, dims, jnp.float32)
    if pieces:
        values = values * shard_levels(own_key, dims, pieces, -0.22, 0.18)
    return jnp.clip(values, -bound, bound).astype(held_as)


def setup_inputs(seed: int = 0) -> dict:
    seeds = jax.random.split(jax.random.key(seed), 13)
    queries = draw_queries(jax.random.fold_in(seeds[12], 71), 0)
    key_rows = draw_key_rows(jax.random.fold_in(seeds[12], 71), 0)
    values = scatter_about(seeds[2], (REPS, TOKENS, INNER), 1.0, 6.0, ((0, 32), (1, 16)))
    out_grad = scatter_about(seeds[3], (REPS, TOKENS, D), 1.0, 6.0, ((0, 32), (1, 16)))
    clip_count = draw_clip_count(jax.random.fold_in(seeds[12], 71), 0)
    clip_lengths = draw_clip_lengths(jax.random.fold_in(seeds[12], 71), 0)
    adapter_in = scatter_about(seeds[6], (INNER, RANK), 1.0, 4.0, ((0, 16),), jnp.float32)
    adapter_out = scatter_about(seeds[7], (RANK, D), 1.0, 4.0, ((0, 16),), jnp.float32)
    moment_in = scatter_about(seeds[8], (INNER, RANK), 0.5, 3.0, ((0, 16),), jnp.float32)
    square_in = jnp.clip(jnp.exp(math.log(2.0) - 3.6888794 * jax.random.uniform(seeds[9], (INNER, RANK), jnp.float32) ** shard_levels(seeds[9], (INNER, RANK), ((0, 16),), -0.2, 0.2)), 0.05, 2.0)
    moment_out = scatter_about(seeds[10], (RANK, D), 0.5, 3.0, ((0, 16),), jnp.float32)
    square_out = jnp.clip(jnp.exp(math.log(2.0) - 3.6888794 * jax.random.uniform(seeds[11], (RANK, D), jnp.float32) ** shard_levels(seeds[11], (RANK, D), ((0, 16),), -0.2, 0.2)), 0.05, 2.0)
    return {"queries": queries, "key_rows": key_rows, "values": values, "out_grad": out_grad, "clip_count": clip_count, "clip_lengths": clip_lengths, "adapter_in": adapter_in, "adapter_out": adapter_out, "moment_in": moment_in, "square_in": square_in, "moment_out": moment_out, "square_out": square_out}


first_rate = 0.9
second_rate = 0.999
adam_steps = 100.0
adam_epsilon = 1e-08
decay_rate = 0.1

def segment_ids(count, lengths, positions):
    active = (jnp.arange(lengths.shape[0], dtype=jnp.int32) < count).astype(lengths.dtype)
    ends = jnp.cumsum(lengths * active)
    return lax.optimization_barrier(jnp.sum((positions[:, None] >= ends[None, :]).astype(jnp.int32), axis=1))

def attend(query_head, key_head, value_head, segment):
    scores = jnp.dot(query_head, key_head.T, preferred_element_type=jnp.float32) * HD ** (-0.5)
    allowed = segment[:, None] == segment[None, :]
    highest = lax.optimization_barrier(jnp.max(jnp.where(allowed, scores, -jnp.inf), axis=1, keepdims=True))
    exponent = jnp.exp(jnp.where(allowed, scores - highest, -jnp.inf))
    row_total = lax.optimization_barrier(jnp.sum(exponent, axis=1, keepdims=True))
    weights = exponent.astype(jnp.bfloat16)
    mixed = jnp.dot(weights, value_head, preferred_element_type=jnp.float32) / row_total
    return mixed.astype(jnp.bfloat16)

def adamw(param, grad, moment, square):
    momentum = first_rate * moment + (1.0 - first_rate) * grad
    variance = second_rate * square + (1.0 - second_rate) * grad * grad
    first_hat = momentum / (1.0 - first_rate ** adam_steps)
    second_hat = variance / (1.0 - second_rate ** adam_steps)
    update = first_hat / (jnp.sqrt(second_hat) + adam_epsilon) + decay_rate * param
    return (momentum, variance, update)

def reference(queries, key_rows, values, out_grad, clip_count, clip_lengths, adapter_in, adapter_out, moment_in, square_in, moment_out, square_out):
    inner_bf = adapter_in.astype(jnp.bfloat16)
    outer_bf = adapter_out.astype(jnp.bfloat16)
    positions = jnp.arange(TOKENS, dtype=jnp.int32)

    def one_replica(carry, element):
        query_all, key_all, value_all, grad_rows, count, lengths = element
        segment = segment_ids(count, lengths, positions)
        query_heads = query_all.reshape(TOKENS, HEADS, HD).transpose(1, 0, 2)
        key_heads = key_all.reshape(TOKENS, HEADS, HD).transpose(1, 0, 2)
        value_heads = value_all.reshape(TOKENS, HEADS, HD).transpose(1, 0, 2)
        mixed = lax.map(lambda triple: attend(triple[0], triple[1], triple[2], segment), (query_heads, key_heads, value_heads))
        attended = mixed.transpose(1, 0, 2).reshape(TOKENS, INNER)
        live = (segment < lengths.shape[0]).astype(grad_rows.dtype)
        grad_live = grad_rows * live[:, None]
        adapted = (jnp.dot(attended, inner_bf, preferred_element_type=jnp.float32) * INNER ** (-0.5)).astype(jnp.bfloat16)
        slopes = (jnp.dot(grad_live, outer_bf.T, preferred_element_type=jnp.float32) * RANK ** (-0.5)).astype(jnp.bfloat16)
        grad_in = carry[0] + jnp.dot(attended.T, slopes, preferred_element_type=jnp.float32) * INNER ** (-0.5)
        grad_out = carry[1] + jnp.dot(adapted.T, grad_live, preferred_element_type=jnp.float32) * RANK ** (-0.5)
        return ((grad_in, grad_out), None)
    start = (jnp.zeros((INNER, RANK), jnp.float32), jnp.zeros((RANK, D), jnp.float32))
    (grad_in, grad_out), _ = lax.scan(one_replica, start, (queries, key_rows, values, out_grad, clip_count, clip_lengths))
    momentum_in, variance_in, update_in = adamw(adapter_in, grad_in, moment_in, square_in)
    momentum_out, variance_out, update_out = adamw(adapter_out, grad_out, moment_out, square_out)
    return (momentum_in, variance_in, update_in, momentum_out, variance_out, update_out)
```

```python
import functools
import math

import jax
import jax.numpy as jnp
from jax import lax
from jax.experimental import pallas as pl
from jax.experimental.pallas import tpu as pltpu
from jax.sharding import PartitionSpec as P

HD = 128
MAX_CLIPS = 3
MESH = pl.DeviceIdType.MESH

first_rate = 0.9
second_rate = 0.999
adam_steps = 100.0
adam_epsilon = 1e-08
decay_rate = 0.1

EXP2_SCALE = HD ** (-0.5) * math.log2(math.e)
MASK = -131072.0
KEY_CHUNKS = 4


def adamw(param, grad, moment, square):
    momentum = first_rate * moment + (1.0 - first_rate) * grad
    variance = second_rate * square + (1.0 - second_rate) * grad * grad
    first_hat = momentum / (1.0 - first_rate**adam_steps)
    second_hat = variance / (1.0 - second_rate**adam_steps)
    update = first_hat / (jnp.sqrt(second_hat) + adam_epsilon) + decay_rate * param
    return (momentum, variance, update)


def remote(src, dst, send_sem, recv_sem, device):
    return pltpu.make_async_remote_copy(
        src_ref=src,
        dst_ref=dst,
        send_sem=send_sem,
        recv_sem=recv_sem,
        device_id=device,
        device_id_type=MESH,
    )


def each(n, body, start=0):
    def step(i, carry):
        body(i)
        return carry

    lax.fori_loop(start, n, step, 0)


def step_kernel(
    dims,
    count_ref,
    lengths_ref,
    q_hbm,
    k_hbm,
    v_hbm,
    og_hbm,
    ain_hbm,
    aout_hbm,
    gin_ref,
    gout_ref,
    q_all,
    k_all,
    v_all,
    scores_buf,
    high_buf,
    mixed,
    attended,
    og_all,
    ain_own,
    aout_own,
    ain_cast,
    aout_cast,
    ain_all,
    aout_all,
    slopes_all,
    adapted_all,
    summed,
    chip_in,
    in_bufs,
    out_bufs,
    load_sems,
    og_s,
    og_r,
    ad_s,
    ad_r,
    k_s,
    k_r,
    v_s,
    v_r,
    q_s,
    q_r,
    o_s,
    o_r,
    ai_s,
    ai_r,
    ao_s,
    ao_r,
    sl_s,
    sl_r,
    chip_s,
    chip_r,
    az_s,
    az_r,
    cz_s,
    cz_r,
    half_s,
    half_r,
    in_sems,
    out_sems,
):
    tok, groups, nz, ny = dims
    chips = groups // 2
    tokens = tok * groups
    rank = ain_hbm.shape[1]
    inner = HD * groups
    me = lax.axis_index("sp")
    rep = lax.axis_index("rep")
    chip = me // 2
    core = lax.rem(me, 2)
    partner = me + 1 - 2 * core
    z = rep // ny
    y = lax.rem(rep, ny)

    def rows(s):
        return pl.ds(pl.multiple_of(s * tok, tok), tok)

    def lanes(s):
        return pl.ds(pl.multiple_of(s * HD, HD), HD)

    def same_core(i):
        return 2 * lax.rem(chip + i, chips) + core

    barrier = pltpu.get_barrier_semaphore()

    def greet_sp(i):
        pl.semaphore_signal(
            barrier, inc=1, device_id={"sp": lax.rem(me + i, groups)}, device_id_type=MESH
        )

    def greet_z(i):
        pl.semaphore_signal(
            barrier,
            inc=1,
            device_id={"rep": lax.rem(z + i, nz) * ny + y},
            device_id_type=MESH,
        )

    def greet_y(i):
        pl.semaphore_signal(
            barrier,
            inc=1,
            device_id={"rep": z * ny + lax.rem(y + i, ny)},
            device_id_type=MESH,
        )

    each(groups, greet_sp, 1)
    each(nz, greet_z, 1)
    each(ny, greet_y, 1)

    load_og = pltpu.make_async_copy(og_hbm.at[0], og_all.at[core], load_sems.at[0])
    load_ain = pltpu.make_async_copy(ain_hbm, ain_own, load_sems.at[1])
    load_aout = pltpu.make_async_copy(aout_hbm, aout_own, load_sems.at[2])
    load_ain.start()
    load_aout.start()
    load_og.start()
    ends = []
    for j in range(MAX_CLIPS):
        length = jnp.where(count_ref[0] > j, lengths_ref[0, j], 0)
        ends.append(length if j == 0 else ends[-1] + length)

    def segment(positions):
        return sum((positions >= e).astype(jnp.int32) for e in ends)

    block = 2 * tok

    def features(b):
        r = pl.ds(pl.multiple_of(b * block, block), block)
        at = b * block + lax.broadcasted_iota(jnp.int32, (block, HD), 0)
        feature = lax.broadcasted_iota(jnp.int32, (block, HD), 1)
        seg = segment(at)
        same = seg == feature
        k_all[r, HD:] = jnp.where(same, 1.0, 0.0).astype(jnp.bfloat16)
        other = jnp.where(feature <= MAX_CLIPS, MASK, 0.0)
        q_all[r, HD:] = jnp.where(same, 0.0, other).astype(jnp.bfloat16)

    each(chips, features)
    mine = me * tok + lax.broadcasted_iota(jnp.int32, (tok, rank), 0)
    live = segment(mine) < MAX_CLIPS
    load_ain.wait()
    load_aout.wait()
    ain_cast[...] = ain_own[...].astype(jnp.bfloat16)
    aout_cast[...] = aout_own[...].astype(jnp.bfloat16)
    pl.semaphore_wait(barrier, groups + nz + ny - 3)

    half = groups // 2
    in_rows = HD // nz
    out_cols = gout_ref.shape[1] // nz
    side = me // half
    z_cols = pl.ds(pl.multiple_of(z * out_cols, out_cols), out_cols)
    z_rows = pl.ds(pl.multiple_of(z * in_rows, in_rows), in_rows)

    def share_device(i):
        return 2 * lax.rem(chip + i, chips) + side

    def aout_share(device):
        return remote(
            aout_cast.at[:, z_cols],
            aout_all.at[me, :, z_cols],
            ao_s.at[device],
            ao_r.at[me],
            {"sp": device},
        )

    def ain_share(device):
        return remote(
            ain_cast.at[z_rows], ain_all.at[me, z_rows], ai_s.at[device], ai_r.at[me], {"sp": device}
        )

    @pl.when(core == side)
    def _():
        pltpu.make_async_copy(
            aout_cast.at[:, z_cols], aout_all.at[me, :, z_cols], ao_r.at[me]
        ).start()
        pltpu.make_async_copy(ain_cast.at[z_rows], ain_all.at[me, z_rows], ai_r.at[me]).start()

    @pl.when(core != side)
    def _():
        aout_share(partner).start()
        ain_share(partner).start()

    def send_share(i):
        aout_share(share_device(i)).start()
        ain_share(share_device(i)).start()

    each(chips, send_share, 1)

    def head_to(src, dst, s, r, device):
        return remote(
            src.at[0, :, lanes(device)],
            dst.at[rows(me), pl.ds(0, HD)],
            s.at[device],
            r.at[me],
            {"sp": device},
        )

    def own_head(src, dst, r):
        return pltpu.make_async_copy(
            src.at[0, :, lanes(me)], dst.at[rows(me), pl.ds(0, HD)], r.at[me]
        )

    def to_peer(i):
        return lax.rem(me - i + groups, groups)

    own_head(k_hbm, k_all, k_r).start()
    each(groups, lambda i: head_to(k_hbm, k_all, k_s, k_r, to_peer(i)).start(), 1)
    own_head(v_hbm, v_all, v_r).start()
    each(groups, lambda i: head_to(v_hbm, v_all, v_s, v_r, to_peer(i)).start(), 1)
    own_head(q_hbm, q_all, q_r).start()
    each(groups, lambda i: head_to(q_hbm, q_all, q_s, q_r, to_peer(i)).start(), 1)

    send_og = remote(og_hbm.at[0], og_all.at[core], og_s, og_r, {"sp": partner})
    send_og.start()

    owners = pl.ds(pl.multiple_of(core * half, half), half)

    def wait_share(i):
        owner = core * half + i
        remote(
            aout_cast.at[:, z_cols],
            aout_all.at[owner, :, z_cols],
            ao_s.at[owner],
            ao_r.at[owner],
            {"sp": partner},
        ).wait_recv()
        remote(
            ain_cast.at[z_rows],
            ain_all.at[owner, z_rows],
            ai_s.at[owner],
            ai_r.at[owner],
            {"sp": partner},
        ).wait_recv()

    each(half, wait_share)

    def z_peer(i):
        return lax.rem(z + i, nz)

    def aout_along(p, origin):
        cols = pl.ds(pl.multiple_of(origin * out_cols, out_cols), out_cols)
        part = aout_all.at[owners, :, cols]
        return remote(part, part, az_s.at[p], az_r.at[origin], {"rep": p * ny + y})

    def ain_along(p, origin):
        lines = pl.ds(pl.multiple_of(origin * in_rows, in_rows), in_rows)
        part = ain_all.at[owners, lines]
        return remote(part, part, cz_s.at[p], cz_r.at[origin], {"rep": p * ny + y})

    def send_along(i):
        aout_along(z_peer(i), z).start()
        ain_along(z_peer(i), z).start()

    each(nz, send_along, 1)

    def wait_along(i):
        aout_along(z_peer(i), z_peer(i)).wait_recv()
        ain_along(z_peer(i), z_peer(i)).wait_recv()

    each(nz, wait_along, 1)
    swap_out = remote(
        aout_all.at[owners], aout_all.at[owners], half_s.at[0], half_r.at[0], {"sp": partner}
    )
    swap_in = remote(
        ain_all.at[owners], ain_all.at[owners], half_s.at[1], half_r.at[1], {"sp": partner}
    )
    swap_out.start()
    swap_in.start()
    swap_out.wait_recv()
    swap_in.wait_recv()
    load_og.wait()

    outer = jnp.concatenate([aout_all[i].astype(jnp.float32) for i in range(groups)], axis=0)
    slopes = lax.dot_general(
        og_all[core],
        outer.astype(jnp.bfloat16),
        (((1,), (1,)), ((), ())),
        preferred_element_type=jnp.float32,
    ) * rank ** (-0.5)
    slopes_all[rows(me)] = jnp.where(live, slopes, 0.0).astype(jnp.bfloat16)

    def slopes_to(owner, device, slot):
        return remote(
            slopes_all.at[rows(owner)],
            slopes_all.at[rows(owner)],
            sl_s.at[slot],
            sl_r.at[owner],
            {"sp": device},
        )

    slopes_to(me, partner, 0).start()
    each(chips, lambda i: slopes_to(me, same_core(i), i).start(), 1)

    def wait_head(dst, r, s, peer):
        remote(
            dst.at[rows(peer), pl.ds(0, HD)],
            dst.at[rows(peer), pl.ds(0, HD)],
            s.at[peer],
            r.at[peer],
            {"sp": partner},
        ).wait_recv()

    each(groups, lambda i: wait_head(k_all, k_r, k_s, i))
    each(groups, lambda i: wait_head(v_all, v_r, v_s, i))

    def chip_of(i):
        return lax.rem(chip + i, chips)

    def block_rows(i):
        return pl.ds(pl.multiple_of(chip_of(i) * block, block), block)

    def wait_queries(i):
        wait_head(q_all, q_r, q_s, 2 * chip_of(i))
        wait_head(q_all, q_r, q_s, 2 * chip_of(i) + 1)

    width = tokens // KEY_CHUNKS

    def scores(i, slot):
        query = q_all[block_rows(i), :]
        high = None
        for c in range(KEY_CHUNKS):
            s = lax.dot_general(
                query,
                k_all[c * width : (c + 1) * width, :],
                (((1,), (1,)), ((), ())),
                preferred_element_type=jnp.float32,
            )
            scores_buf[slot, :, c * width : (c + 1) * width] = s
            for j in range(width // HD):
                piece = s[:, j * HD : (j + 1) * HD]
                high = piece if high is None else jnp.maximum(high, piece)
        high_buf[slot] = jnp.broadcast_to(jnp.max(high, axis=1, keepdims=True), (block, HD))

    def finish(i, slot):
        high = high_buf[slot][:, :1]
        total = None
        row_total = None
        for c in range(KEY_CHUNKS):
            s = scores_buf[slot, :, c * width : (c + 1) * width]
            exponent = jnp.exp2((s - high) * EXP2_SCALE)
            for j in range(width // HD):
                piece = exponent[:, j * HD : (j + 1) * HD]
                row_total = piece if row_total is None else row_total + piece
            term = jnp.dot(
                exponent.astype(jnp.bfloat16),
                v_all[c * width : (c + 1) * width, :],
                preferred_element_type=jnp.float32,
            )
            total = term if total is None else total + term
        row_total = jnp.sum(row_total, axis=1, keepdims=True)
        mixed[block_rows(i), :] = (total / row_total).astype(jnp.bfloat16)

    def mixed_to(device):
        return remote(
            mixed.at[rows(device)],
            attended.at[:, lanes(me)],
            o_s.at[device],
            o_r.at[me],
            {"sp": device},
        )

    def own_mixed():
        return pltpu.make_async_copy(mixed.at[rows(me)], attended.at[:, lanes(me)], o_r.at[me])

    def give_back(i):
        for c in range(2):
            device = 2 * chip_of(i) + c

            @pl.when(device == me)
            def _():
                own_mixed().start()

            @pl.when(device != me)
            def _():
                mixed_to(device).start()

    wait_queries(0)
    scores(0, 0)

    def two_blocks(t):
        i = 2 * t
        wait_queries(i + 1)
        scores(i + 1, 1)
        finish(i, 0)
        give_back(i)
        wait_queries(i + 2)
        scores(i + 2, 0)
        finish(i + 1, 1)
        give_back(i + 1)

    each(chips // 2 - 1, two_blocks)

    def forward_slopes(i):
        owner = same_core(i)
        slopes_to(owner, partner, chips + i).wait_recv()
        slopes_to(owner, partner, chips + i).start()

    each(chips, forward_slopes, 1)

    wait_queries(chips - 1)
    scores(chips - 1, 1)
    finish(chips - 2, 0)
    give_back(chips - 2)
    finish(chips - 1, 1)
    give_back(chips - 1)

    each(chips, lambda i: slopes_to(2 * i + 1 - core, partner, 0).wait_recv())
    grad_in = lax.dot_general(
        mixed[...], slopes_all[...], (((0,), (0,)), ((), ())), preferred_element_type=jnp.float32
    ) * inner ** (-0.5)
    out_tiles = out_cols // HD

    def y_peer(i):
        return lax.rem(y + i, ny)

    class Replicas:
        def __init__(self, bufs, sems):
            self.pack, self.z_in, self.y_out, self.y_in, self.z_out, self.whole = bufs
            self.zi_s, self.zi_r, self.y_s, self.y_r, self.zo_s, self.zo_r = sems

        def z_copy(self, p, origin):
            return remote(
                self.pack.at[p],
                self.z_in.at[origin],
                self.zi_s.at[p],
                self.zi_r.at[origin],
                {"rep": p * ny + y},
            )

        def y_copy(self, p, origin):
            return remote(
                self.y_out,
                self.y_in.at[origin],
                self.y_s.at[p],
                self.y_r.at[origin],
                {"rep": z * ny + p},
            )

        def back_copy(self, p, origin):
            return remote(
                self.z_out,
                self.whole.at[origin],
                self.zo_s.at[p],
                self.zo_r.at[origin],
                {"rep": p * ny + y},
            )

        def start(self):
            each(nz, lambda i: self.z_copy(z_peer(i), z).start(), 1)
            self.z_in[z] = self.pack[z]

        def across(self):
            each(nz, lambda i: self.z_copy(z_peer(i), z_peer(i)).wait_recv(), 1)
            total = self.z_in[0]
            for p in range(1, nz):
                total = total + self.z_in[p]
            self.y_out[...] = total
            each(ny, lambda i: self.y_copy(y_peer(i), y).start(), 1)
            self.y_in[y] = total

        def back(self):
            each(ny, lambda i: self.y_copy(y_peer(i), y_peer(i)).wait_recv(), 1)
            total = self.y_in[0]
            for p in range(1, ny):
                total = total + self.y_in[p]
            self.z_out[...] = total
            each(nz, lambda i: self.back_copy(z_peer(i), z).start(), 1)
            self.whole[z] = total

        def arrive(self):
            each(nz, lambda i: self.back_copy(z_peer(i), z_peer(i)).wait_recv(), 1)

        def sent(self):
            each(nz, lambda i: self.z_copy(z_peer(i), z).wait_send(), 1)
            each(ny, lambda i: self.y_copy(y_peer(i), y).wait_send(), 1)
            each(nz, lambda i: self.back_copy(z_peer(i), z).wait_send(), 1)

    sum_in = Replicas(in_bufs, in_sems)
    sum_out = Replicas(out_bufs, out_sems)
    for p in range(nz):
        sum_in.pack[p] = grad_in[p * in_rows : (p + 1) * in_rows]
    sum_in.start()

    def wait_mixed(i):
        remote(
            mixed.at[rows(i)], attended.at[:, lanes(i)], o_s.at[i], o_r.at[i], {"sp": partner}
        ).wait_recv()

    each(groups, wait_mixed)
    adapted = jnp.dot(
        attended[...], ain_all[...].reshape(inner, rank), preferred_element_type=jnp.float32
    )
    adapted_all[core] = jnp.where(live, adapted * inner ** (-0.5), 0.0).astype(jnp.bfloat16)
    send_adapted = remote(adapted_all.at[core], adapted_all.at[core], ad_s, ad_r, {"sp": partner})
    send_adapted.start()
    sum_in.across()
    send_og.wait_recv()
    send_adapted.wait_recv()
    term_out = lax.dot_general(
        adapted_all[...].reshape(block, rank),
        og_all[...].reshape(block, og_all.shape[2]),
        (((0,), (0,)), ((), ())),
        preferred_element_type=jnp.float32,
    ) * rank ** (-0.5)
    depth = rank // groups

    for j in range(chips):
        at = 2 * j * depth
        summed[j] = jnp.where(
            core == 0, term_out[at : at + depth], term_out[at + depth : at + 2 * depth]
        )

    def chunk_to(i):
        j = lax.rem(chip + i, chips)
        return remote(
            summed.at[j], chip_in.at[chip], chip_s.at[j], chip_r.at[chip], {"sp": 2 * j + core}
        )

    each(chips, lambda i: chunk_to(i).start(), 1)
    chip_in[chip] = summed[chip]

    def wait_chunk(i):
        j = lax.rem(chip + i, chips)
        remote(
            summed.at[j], chip_in.at[j], chip_s.at[j], chip_r.at[j], {"sp": 2 * j + core}
        ).wait_recv()

    sum_in.back()
    each(chips, wait_chunk, 1)
    grad_out = chip_in[0]
    for j in range(1, chips):
        grad_out = grad_out + chip_in[j]

    for p in range(nz):
        for t in range(out_tiles):
            at = p * out_cols + t * HD
            sum_out.pack[p, t * 8 : (t + 1) * 8] = grad_out[:, at : at + HD]
    sum_out.start()
    sum_in.arrive()
    for p in range(nz):
        gin_ref[p * in_rows : (p + 1) * in_rows] = sum_in.whole[p]
    sum_out.across()


    @pl.when(core != side)
    def _():
        aout_share(partner).wait_send()
        ain_share(partner).wait_send()

    def sent_to_chips(i):
        aout_share(share_device(i)).wait_send()
        ain_share(share_device(i)).wait_send()
        slopes_to(me, same_core(i), i).wait_send()
        slopes_to(same_core(i), partner, chips + i).wait_send()
        chunk_to(i).wait_send()

    each(chips, sent_to_chips, 1)
    slopes_to(me, partner, 0).wait_send()
    send_og.wait_send()
    send_adapted.wait_send()
    swap_out.wait_send()
    swap_in.wait_send()

    def sent_along(i):
        aout_along(z_peer(i), z).wait_send()
        ain_along(z_peer(i), z).wait_send()

    each(nz, sent_along, 1)

    def sent_to_group(i):
        peer = to_peer(i)
        head_to(k_hbm, k_all, k_s, k_r, peer).wait_send()
        head_to(v_hbm, v_all, v_s, v_r, peer).wait_send()
        head_to(q_hbm, q_all, q_s, q_r, peer).wait_send()
        mixed_to(peer).wait_send()

    each(groups, sent_to_group, 1)
    sum_out.back()
    sum_in.sent()
    sum_out.sent()
    sum_out.arrive()
    for p in range(nz):
        for t in range(out_tiles):
            at = p * out_cols + t * HD
            gout_ref[:, at : at + HD] = sum_out.whole[p, t * 8 : (t + 1) * 8]


def adamw_kernel(*refs):
    ins, outs = refs[:8], refs[8:]
    for at in range(2):
        param, grad, moment, square = (r[...] for r in ins[4 * at : 4 * at + 4])
        for ref, value in zip(outs[3 * at : 3 * at + 3], adamw(param, grad, moment, square)):
            ref[...] = value


def per_device(
    queries,
    key_rows,
    values,
    out_grad,
    clip_count,
    clip_lengths,
    adapter_in,
    adapter_out,
    moment_in,
    square_in,
    moment_out,
    square_out,
):
    tok = queries.shape[1]
    width = out_grad.shape[2]
    rank = adapter_in.shape[1]
    groups = lax.axis_size("sp")
    chips = groups // 2
    reps = lax.axis_size("rep")
    ny = 4 if reps % 4 == 0 and reps > 4 else 1
    nz = reps // ny
    tokens = tok * groups
    depth = rank // groups
    in_lines, out_lines = HD // nz, (width // nz // HD) * 8
    bf16, f32 = jnp.bfloat16, jnp.float32
    vmem = pl.BlockSpec(memory_space=pltpu.VMEM)
    smem = pl.BlockSpec(memory_space=pltpu.SMEM)
    hbm = pl.BlockSpec(memory_space=pl.ANY)
    dma = pltpu.SemaphoreType.DMA

    def sum_bufs(lines):
        return [
            pltpu.VMEM((nz, lines, HD), f32),
            pltpu.VMEM((nz, lines, HD), f32),
            pltpu.VMEM((lines, HD), f32),
            pltpu.VMEM((ny, lines, HD), f32),
            pltpu.VMEM((lines, HD), f32),
            pltpu.VMEM((nz, lines, HD), f32),
        ]

    sum_sems = [dma((n,)) for n in (nz, nz, ny, ny, nz, nz)]
    grad_in, grad_out = pl.pallas_call(
        functools.partial(step_kernel, (tok, groups, nz, ny)),
        name="adapter_step",
        out_shape=(
            jax.ShapeDtypeStruct((HD, rank), f32),
            jax.ShapeDtypeStruct((depth, width), f32),
        ),
        in_specs=[smem, smem, hbm, hbm, hbm, hbm, hbm, hbm],
        out_specs=(vmem, vmem),
        scratch_shapes=[
            pltpu.VMEM((tokens, 2 * HD), bf16),
            pltpu.VMEM((tokens, 2 * HD), bf16),
            pltpu.VMEM((tokens, HD), bf16),
            pltpu.VMEM((2, 2 * tok, tokens), f32),
            pltpu.VMEM((2, 2 * tok, HD), f32),
            pltpu.VMEM((tokens, HD), bf16),
            pltpu.VMEM((tok, groups * HD), bf16),
            pltpu.VMEM((2, tok, width), bf16),
            pltpu.VMEM((HD, rank), f32),
            pltpu.VMEM((depth, width), f32),
            pltpu.VMEM((HD, rank), bf16),
            pltpu.VMEM((depth, width), bf16),
            pltpu.VMEM((groups, HD, rank), bf16),
            pltpu.VMEM((groups, depth, width), bf16),
            pltpu.VMEM((tokens, rank), bf16),
            pltpu.VMEM((2, tok, rank), bf16),
            pltpu.VMEM((chips, depth, width), f32),
            pltpu.VMEM((chips, depth, width), f32),
            sum_bufs(in_lines),
            sum_bufs(out_lines),
            dma((3,)),
        ]
        + [dma(())] * 4
        + [dma((groups,))] * 14
        + [dma((chips,))] * 2
        + [dma((nz,))] * 4
        + [dma((2,))] * 2
        + [sum_sems, sum_sems],
        compiler_params=pltpu.CompilerParams(
            collective_id=0, has_side_effects=True, vmem_limit_bytes=60 * 2**20
        ),
    )(
        clip_count,
        clip_lengths,
        queries,
        key_rows,
        values,
        out_grad,
        adapter_in,
        adapter_out,
    )
    return tuple(
        pl.pallas_call(
            adamw_kernel,
            name="adamw",
            out_shape=[jax.ShapeDtypeStruct(a.shape, f32) for a in [grad_in] * 3 + [grad_out] * 3],
            in_specs=[vmem] * 8,
            out_specs=[vmem] * 6,
        )(
            adapter_in,
            grad_in,
            moment_in,
            square_in,
            adapter_out,
            grad_out,
            moment_out,
            square_out,
        )
    )


def solution(mesh):
    placed = (
        P("rep", "sp", None),
        P("rep", "sp", None),
        P("rep", "sp", None),
        P("rep", "sp", None),
        P("rep"),
        P("rep", None),
        P("sp", None),
        P("sp", None),
        P("sp", None),
        P("sp", None),
        P("sp", None),
        P("sp", None),
    )
    return jax.shard_map(
        per_device,
        mesh=mesh,
        in_specs=placed,
        out_specs=(
            P("sp", None),
            P("sp", None),
            P("sp", None),
            P("sp", None),
            P("sp", None),
            P("sp", None),
        ),
        check_vma=False,
    )
```

```python
import functools
import math

import jax
import jax.numpy as jnp
from jax import lax
from jax.experimental import pallas as pl
from jax.experimental.pallas import tpu as pltpu
from jax.sharding import PartitionSpec as P

HD = 128
MAX_CLIPS = 3
MESH = pl.DeviceIdType.MESH

first_rate = 0.9
second_rate = 0.999
adam_steps = 100.0
adam_epsilon = 1e-08
decay_rate = 0.1

EXP2_SCALE = HD ** (-0.5) * math.log2(math.e)
MASK = -131072.0
KEY_CHUNKS = 4


def adamw(param, grad, moment, square):
    momentum = first_rate * moment + (1.0 - first_rate) * grad
    variance = second_rate * square + (1.0 - second_rate) * grad * grad
    first_hat = momentum / (1.0 - first_rate**adam_steps)
    second_hat = variance / (1.0 - second_rate**adam_steps)
    update = first_hat / (jnp.sqrt(second_hat) + adam_epsilon) + decay_rate * param
    return (momentum, variance, update)


def remote(src, dst, send_sem, recv_sem, device):
    return pltpu.make_async_remote_copy(
        src_ref=src,
        dst_ref=dst,
        send_sem=send_sem,
        recv_sem=recv_sem,
        device_id=device,
        device_id_type=MESH,
    )


def each(n, body, start=0):
    def step(i, carry):
        body(i)
        return carry

    lax.fori_loop(start, n, step, 0)


def step_kernel(
    dims,
    count_ref,
    lengths_ref,
    q_hbm,
    k_hbm,
    v_hbm,
    og_hbm,
    ain_hbm,
    aout_hbm,
    gin_ref,
    gout_ref,
    q_all,
    k_all,
    v_all,
    scores_buf,
    high_buf,
    mixed,
    attended,
    og_all,
    ain_own,
    aout_own,
    ain_cast,
    aout_cast,
    ain_all,
    aout_all,
    slopes_all,
    adapted_all,
    summed,
    chip_in,
    z_first,
    z_first_in,
    tiles,
    tile_in,
    in_bufs,
    out_bufs,
    load_sems,
    og_s,
    og_r,
    ad_s,
    ad_r,
    k_s,
    k_r,
    v_s,
    v_r,
    q_s,
    q_r,
    o_s,
    o_r,
    ai_s,
    ai_r,
    ao_s,
    ao_r,
    sl_s,
    sl_r,
    chip_s,
    chip_r,
    ti_s,
    ti_r,
    zf_s,
    zf_r,
    az_s,
    az_r,
    cz_s,
    cz_r,
    half_s,
    half_r,
    in_sems,
    out_sems,
):
    tok, groups, nz, ny = dims
    chips = groups // 2
    tokens = tok * groups
    rank = ain_hbm.shape[1]
    inner = HD * groups
    me = lax.axis_index("sp")
    rep = lax.axis_index("rep")
    chip = me // 2
    core = lax.rem(me, 2)
    partner = me + 1 - 2 * core
    z = rep // ny
    y = lax.rem(rep, ny)

    def rows(s):
        return pl.ds(pl.multiple_of(s * tok, tok), tok)

    def lanes(s):
        return pl.ds(pl.multiple_of(s * HD, HD), HD)

    def same_core(i):
        return 2 * lax.rem(chip + i, chips) + core

    barrier = pltpu.get_barrier_semaphore()

    def greet_sp(i):
        pl.semaphore_signal(
            barrier, inc=1, device_id={"sp": lax.rem(me + i, groups)}, device_id_type=MESH
        )

    def greet_z(i):
        pl.semaphore_signal(
            barrier,
            inc=1,
            device_id={"rep": lax.rem(z + i, nz) * ny + y},
            device_id_type=MESH,
        )

    def greet_y(i):
        pl.semaphore_signal(
            barrier,
            inc=1,
            device_id={"rep": z * ny + lax.rem(y + i, ny)},
            device_id_type=MESH,
        )

    each(groups, greet_sp, 1)
    each(nz, greet_z, 1)
    each(ny, greet_y, 1)

    load_og = pltpu.make_async_copy(og_hbm.at[0], og_all.at[core], load_sems.at[0])
    load_ain = pltpu.make_async_copy(ain_hbm, ain_own, load_sems.at[1])
    load_aout = pltpu.make_async_copy(aout_hbm, aout_own, load_sems.at[2])
    load_ain.start()
    load_aout.start()
    load_og.start()
    pl.semaphore_wait(barrier, groups + nz + ny - 3)

    def head_to(src, dst, s, r, device):
        return remote(
            src.at[0, :, lanes(device)],
            dst.at[rows(me), pl.ds(0, HD)],
            s.at[device],
            r.at[me],
            {"sp": device},
        )

    def own_head(src, dst, r):
        return pltpu.make_async_copy(
            src.at[0, :, lanes(me)], dst.at[rows(me), pl.ds(0, HD)], r.at[me]
        )

    def to_peer(i):
        return lax.rem(me - i + groups, groups)

    own_head(k_hbm, k_all, k_r).start()
    each(groups, lambda i: head_to(k_hbm, k_all, k_s, k_r, to_peer(i)).start(), 1)

    half = groups // 2
    in_rows = HD // nz
    out_cols = gout_ref.shape[1] // nz
    side = me // half
    z_cols = pl.ds(pl.multiple_of(z * out_cols, out_cols), out_cols)
    z_rows = pl.ds(pl.multiple_of(z * in_rows, in_rows), in_rows)

    def share_device(i):
        return 2 * lax.rem(chip + i, chips) + side

    def aout_share(device):
        return remote(
            aout_cast.at[:, z_cols],
            aout_all.at[me, :, z_cols],
            ao_s.at[device],
            ao_r.at[me],
            {"sp": device},
        )

    def ain_share(device):
        return remote(
            ain_cast.at[z_rows], ain_all.at[me, z_rows], ai_s.at[device], ai_r.at[me], {"sp": device}
        )

    load_ain.wait()
    load_aout.wait()
    ain_cast[...] = ain_own[...].astype(jnp.bfloat16)
    aout_cast[...] = aout_own[...].astype(jnp.bfloat16)

    @pl.when(core == side)
    def _():
        pltpu.make_async_copy(
            aout_cast.at[:, z_cols], aout_all.at[me, :, z_cols], ao_r.at[me]
        ).start()
        pltpu.make_async_copy(ain_cast.at[z_rows], ain_all.at[me, z_rows], ai_r.at[me]).start()

    @pl.when(core != side)
    def _():
        aout_share(partner).start()
        ain_share(partner).start()

    def send_share(i):
        aout_share(share_device(i)).start()
        ain_share(share_device(i)).start()

    each(chips, send_share, 1)
    own_head(v_hbm, v_all, v_r).start()
    each(groups, lambda i: head_to(v_hbm, v_all, v_s, v_r, to_peer(i)).start(), 1)
    own_head(q_hbm, q_all, q_r).start()
    each(groups, lambda i: head_to(q_hbm, q_all, q_s, q_r, to_peer(i)).start(), 1)

    send_og = remote(og_hbm.at[0], og_all.at[core], og_s, og_r, {"sp": partner})
    send_og.start()

    ends = []
    for j in range(MAX_CLIPS):
        length = jnp.where(count_ref[0] > j, lengths_ref[0, j], 0)
        ends.append(length if j == 0 else ends[-1] + length)

    def segment(positions):
        return sum((positions >= e).astype(jnp.int32) for e in ends)

    block = 2 * tok

    def features(b):
        r = pl.ds(pl.multiple_of(b * block, block), block)
        at = b * block + lax.broadcasted_iota(jnp.int32, (block, HD), 0)
        feature = lax.broadcasted_iota(jnp.int32, (block, HD), 1)
        seg = segment(at)
        same = seg == feature
        k_all[r, HD:] = jnp.where(same, 1.0, 0.0).astype(jnp.bfloat16)
        other = jnp.where(feature <= MAX_CLIPS, MASK, 0.0)
        q_all[r, HD:] = jnp.where(same, 0.0, other).astype(jnp.bfloat16)

    each(chips, features)
    mine = me * tok + lax.broadcasted_iota(jnp.int32, (tok, rank), 0)
    live = segment(mine) < MAX_CLIPS

    owners = pl.ds(pl.multiple_of(core * half, half), half)

    def wait_share(i):
        owner = core * half + i
        remote(
            aout_cast.at[:, z_cols],
            aout_all.at[owner, :, z_cols],
            ao_s.at[owner],
            ao_r.at[owner],
            {"sp": partner},
        ).wait_recv()
        remote(
            ain_cast.at[z_rows],
            ain_all.at[owner, z_rows],
            ai_s.at[owner],
            ai_r.at[owner],
            {"sp": partner},
        ).wait_recv()

    each(half, wait_share)

    def z_peer(i):
        return lax.rem(z + i, nz)

    def aout_along(p, origin):
        cols = pl.ds(pl.multiple_of(origin * out_cols, out_cols), out_cols)
        part = aout_all.at[owners, :, cols]
        return remote(part, part, az_s.at[p], az_r.at[origin], {"rep": p * ny + y})

    def ain_along(p, origin):
        lines = pl.ds(pl.multiple_of(origin * in_rows, in_rows), in_rows)
        part = ain_all.at[owners, lines]
        return remote(part, part, cz_s.at[p], cz_r.at[origin], {"rep": p * ny + y})

    def send_along(i):
        aout_along(z_peer(i), z).start()
        ain_along(z_peer(i), z).start()

    each(nz, send_along, 1)

    def wait_along(i):
        aout_along(z_peer(i), z_peer(i)).wait_recv()
        ain_along(z_peer(i), z_peer(i)).wait_recv()

    swap_out = remote(
        aout_all.at[owners], aout_all.at[owners], half_s.at[0], half_r.at[0], {"sp": partner}
    )
    swap_in = remote(
        ain_all.at[owners], ain_all.at[owners], half_s.at[1], half_r.at[1], {"sp": partner}
    )

    def slopes_to(owner, device, slot):
        return remote(
            slopes_all.at[rows(owner)],
            slopes_all.at[rows(owner)],
            sl_s.at[slot],
            sl_r.at[owner],
            {"sp": device},
        )

    def change_cores():
        each(nz, wait_along, 1)
        swap_out.start()
        swap_in.start()

    def spread_slopes():
        swap_out.wait_recv()
        swap_in.wait_recv()
        load_og.wait()
        outer = jnp.concatenate([aout_all[i].astype(jnp.float32) for i in range(groups)], axis=0)
        slopes = lax.dot_general(
            og_all[core],
            outer.astype(jnp.bfloat16),
            (((1,), (1,)), ((), ())),
            preferred_element_type=jnp.float32,
        ) * rank ** (-0.5)
        slopes_all[rows(me)] = jnp.where(live, slopes, 0.0).astype(jnp.bfloat16)

        slopes_to(me, partner, 0).start()
        each(chips, lambda i: slopes_to(me, same_core(i), i).start(), 1)

    def wait_head(dst, r, s, peer):
        remote(
            dst.at[rows(peer), pl.ds(0, HD)],
            dst.at[rows(peer), pl.ds(0, HD)],
            s.at[peer],
            r.at[peer],
            {"sp": partner},
        ).wait_recv()

    each(groups, lambda i: wait_head(k_all, k_r, k_s, i))
    each(groups, lambda i: wait_head(v_all, v_r, v_s, i))

    def chip_of(i):
        return lax.rem(chip + i, chips)

    def block_rows(i):
        return pl.ds(pl.multiple_of(chip_of(i) * block, block), block)

    def wait_queries(i):
        wait_head(q_all, q_r, q_s, 2 * chip_of(i))
        wait_head(q_all, q_r, q_s, 2 * chip_of(i) + 1)

    width = tokens // KEY_CHUNKS

    def scores(i, slot):
        query = q_all[block_rows(i), :]
        high = None
        for c in range(KEY_CHUNKS):
            s = lax.dot_general(
                query,
                k_all[c * width : (c + 1) * width, :],
                (((1,), (1,)), ((), ())),
                preferred_element_type=jnp.float32,
            )
            scores_buf[slot, :, c * width : (c + 1) * width] = s
            for j in range(width // HD):
                piece = s[:, j * HD : (j + 1) * HD]
                high = piece if high is None else jnp.maximum(high, piece)
        high_buf[slot] = jnp.broadcast_to(jnp.max(high, axis=1, keepdims=True), (block, HD))

    def finish(i, slot):
        high = high_buf[slot][:, :1]
        total = None
        row_total = None
        for c in range(KEY_CHUNKS):
            s = scores_buf[slot, :, c * width : (c + 1) * width]
            exponent = jnp.exp2((s - high) * EXP2_SCALE)
            for j in range(width // HD):
                piece = exponent[:, j * HD : (j + 1) * HD]
                row_total = piece if row_total is None else row_total + piece
            term = jnp.dot(
                exponent.astype(jnp.bfloat16),
                v_all[c * width : (c + 1) * width, :],
                preferred_element_type=jnp.float32,
            )
            total = term if total is None else total + term
        row_total = jnp.sum(row_total, axis=1, keepdims=True)
        mixed[block_rows(i), :] = (total / row_total).astype(jnp.bfloat16)

    def mixed_to(device):
        return remote(
            mixed.at[rows(device)],
            attended.at[:, lanes(me)],
            o_s.at[device],
            o_r.at[me],
            {"sp": device},
        )

    def own_mixed():
        return pltpu.make_async_copy(mixed.at[rows(me)], attended.at[:, lanes(me)], o_r.at[me])

    def give_back(i):
        for c in range(2):
            device = 2 * chip_of(i) + c

            @pl.when(device == me)
            def _():
                own_mixed().start()

            @pl.when(device != me)
            def _():
                mixed_to(device).start()

    wait_queries(0)
    scores(0, 0)

    def two_blocks(t):
        i = 2 * t
        wait_queries(i + 1)
        scores(i + 1, 1)
        finish(i, 0)
        give_back(i)
        wait_queries(i + 2)
        scores(i + 2, 0)
        finish(i + 1, 1)
        give_back(i + 1)

    each(chips // 2 - 2, two_blocks)
    change_cores()
    each(chips // 2 - 1, two_blocks, chips // 2 - 2)
    spread_slopes()

    wait_queries(chips - 1)
    scores(chips - 1, 1)
    finish(chips - 2, 0)
    give_back(chips - 2)
    finish(chips - 1, 1)
    give_back(chips - 1)

    def forward_slopes(i):
        owner = same_core(i)
        slopes_to(owner, partner, chips + i).wait_recv()
        slopes_to(owner, partner, chips + i).start()

    each(chips, forward_slopes, 1)

    out_tiles = out_cols // HD

    def y_peer(i):
        return lax.rem(y + i, ny)

    class Replicas:
        def __init__(self, bufs, sems):
            self.pack, self.z_in, self.y_out, self.y_in, self.z_out, self.whole = bufs
            self.zi_s, self.zi_r, self.y_s, self.y_r, self.zo_s, self.zo_r = sems

        def z_copy(self, p, origin):
            return remote(
                self.pack.at[p],
                self.z_in.at[origin],
                self.zi_s.at[p],
                self.zi_r.at[origin],
                {"rep": p * ny + y},
            )

        def y_copy(self, p, origin):
            return remote(
                self.y_out,
                self.y_in.at[origin],
                self.y_s.at[p],
                self.y_r.at[origin],
                {"rep": z * ny + p},
            )

        def back_copy(self, p, origin):
            return remote(
                self.z_out,
                self.whole.at[origin],
                self.zo_s.at[p],
                self.zo_r.at[origin],
                {"rep": p * ny + y},
            )

        def start(self):
            each(nz, lambda i: self.z_copy(z_peer(i), z).start(), 1)
            self.z_in[z] = self.pack[z]

        def across(self, more=None):
            each(nz, lambda i: self.z_copy(z_peer(i), z_peer(i)).wait_recv(), 1)
            total = self.z_in[0]
            for p in range(1, nz):
                total = total + self.z_in[p]
            if more is not None:
                total = jnp.concatenate([total, more], axis=0)
            self.y_out[...] = total
            each(ny, lambda i: self.y_copy(y_peer(i), y).start(), 1)
            self.y_in[y] = total

        def back(self):
            each(ny, lambda i: self.y_copy(y_peer(i), y_peer(i)).wait_recv(), 1)
            total = self.y_in[0]
            for p in range(1, ny):
                total = total + self.y_in[p]
            self.z_out[...] = total
            each(nz, lambda i: self.back_copy(z_peer(i), z).start(), 1)
            self.whole[z] = total

        def arrive(self):
            each(nz, lambda i: self.back_copy(z_peer(i), z_peer(i)).wait_recv(), 1)

        def sent(self):
            each(nz, lambda i: self.z_copy(z_peer(i), z).wait_send(), 1)
            each(ny, lambda i: self.y_copy(y_peer(i), y).wait_send(), 1)
            each(nz, lambda i: self.back_copy(z_peer(i), z).wait_send(), 1)

    def wait_mixed(i):
        remote(
            mixed.at[rows(i)], attended.at[:, lanes(i)], o_s.at[i], o_r.at[i], {"sp": partner}
        ).wait_recv()

    each(groups, wait_mixed)
    adapted = jnp.dot(
        attended[...], ain_all[...].reshape(inner, rank), preferred_element_type=jnp.float32
    )
    adapted_all[core] = jnp.where(live, adapted * inner ** (-0.5), 0.0).astype(jnp.bfloat16)
    send_adapted = remote(adapted_all.at[core], adapted_all.at[core], ad_s, ad_r, {"sp": partner})
    send_adapted.start()
    send_og.wait_recv()
    send_adapted.wait_recv()
    term_out = lax.dot_general(
        adapted_all[...].reshape(block, rank),
        og_all[...].reshape(block, og_all.shape[2]),
        (((0,), (0,)), ((), ())),
        preferred_element_type=jnp.float32,
    ) * rank ** (-0.5)
    depth = rank // groups

    chip_tiles = out_tiles - 1
    chip_cols = chip_tiles * HD * nz
    for j in range(chips):
        at = 2 * j * depth
        own = jnp.where(
            core == 0, term_out[at : at + depth], term_out[at + depth : at + 2 * depth]
        )
        summed[j] = own[:, :chip_cols]
        for p in range(nz):
            z_first[p, j] = own[:, chip_cols + p * HD : chip_cols + (p + 1) * HD]

    def chunk_to(j, origin):
        return remote(
            summed.at[j],
            chip_in.at[origin],
            chip_s.at[j],
            chip_r.at[origin],
            {"sp": 2 * j + core},
        )

    def z_first_to(p, origin):
        return remote(
            z_first.at[p],
            z_first_in.at[origin],
            zf_s.at[p],
            zf_r.at[origin],
            {"rep": p * ny + y},
        )

    def tile_to(j, origin):
        return remote(
            tiles.at[j], tile_in.at[origin], ti_s.at[j], ti_r.at[origin], {"sp": 2 * j + core}
        )

    each(chips, lambda i: chunk_to(chip_of(i), chip).start(), 1)
    each(nz, lambda i: z_first_to(z_peer(i), z).start(), 1)
    chip_in[chip] = summed[chip]
    z_first_in[z] = z_first[z]

    each(chips, lambda i: slopes_to(2 * i + 1 - core, partner, 0).wait_recv())
    grad_in = lax.dot_general(
        mixed[...], slopes_all[...], (((0,), (0,)), ((), ())), preferred_element_type=jnp.float32
    ) * inner ** (-0.5)
    sum_in = Replicas(in_bufs, in_sems)
    sum_out = Replicas(out_bufs, out_sems)
    for p in range(nz):
        sum_in.pack[p] = grad_in[p * in_rows : (p + 1) * in_rows]
    sum_in.start()

    each(nz, lambda i: z_first_to(z_peer(i), z_peer(i)).wait_recv(), 1)
    own = z_first_in[0]
    for p in range(1, nz):
        own = own + z_first_in[p]
    tiles[...] = own
    each(chips, lambda i: tile_to(chip_of(i), chip).start(), 1)
    tile_in[chip] = tiles[chip]

    each(chips, lambda i: chunk_to(chip_of(i), chip_of(i)).wait_recv(), 1)
    own = chip_in[0]
    for j in range(1, chips):
        own = own + chip_in[j]
    for p in range(nz):
        for t in range(chip_tiles):
            at = (p * chip_tiles + t) * HD
            sum_out.pack[p, t * depth : (t + 1) * depth] = own[:, at : at + HD]
    sum_out.start()
    sum_in.across()
    each(chips, lambda i: tile_to(chip_of(i), chip_of(i)).wait_recv(), 1)
    own = tile_in[0]
    for j in range(1, chips):
        own = own + tile_in[j]
    sum_out.across(own)
    sum_in.back()
    sum_out.back()
    sum_in.arrive()
    for p in range(nz):
        gin_ref[p * in_rows : (p + 1) * in_rows] = sum_in.whole[p]


    @pl.when(core != side)
    def _():
        aout_share(partner).wait_send()
        ain_share(partner).wait_send()

    def sent_to_chips(i):
        aout_share(share_device(i)).wait_send()
        ain_share(share_device(i)).wait_send()
        slopes_to(me, same_core(i), i).wait_send()
        slopes_to(same_core(i), partner, chips + i).wait_send()
        chunk_to(chip_of(i), chip).wait_send()
        tile_to(chip_of(i), chip).wait_send()

    each(chips, sent_to_chips, 1)
    slopes_to(me, partner, 0).wait_send()
    send_og.wait_send()
    send_adapted.wait_send()
    swap_out.wait_send()
    swap_in.wait_send()

    def sent_along(i):
        aout_along(z_peer(i), z).wait_send()
        ain_along(z_peer(i), z).wait_send()
        z_first_to(z_peer(i), z).wait_send()

    each(nz, sent_along, 1)

    def sent_to_group(i):
        peer = to_peer(i)
        head_to(k_hbm, k_all, k_s, k_r, peer).wait_send()
        head_to(v_hbm, v_all, v_s, v_r, peer).wait_send()
        head_to(q_hbm, q_all, q_s, q_r, peer).wait_send()
        mixed_to(peer).wait_send()

    each(groups, sent_to_group, 1)
    sum_in.sent()
    sum_out.sent()
    sum_out.arrive()
    for p in range(nz):
        for t in range(chip_tiles):
            at = (p * chip_tiles + t) * HD
            gout_ref[:, at : at + HD] = sum_out.whole[p, t * depth : (t + 1) * depth]
        at = chip_cols + p * HD
        gout_ref[:, at : at + HD] = sum_out.whole[p, chip_tiles * depth :]


def adamw_kernel(*refs):
    ins, outs = refs[:8], refs[8:]
    for at in range(2):
        param, grad, moment, square = (r[...] for r in ins[4 * at : 4 * at + 4])
        for ref, value in zip(outs[3 * at : 3 * at + 3], adamw(param, grad, moment, square)):
            ref[...] = value


def per_device(
    queries,
    key_rows,
    values,
    out_grad,
    clip_count,
    clip_lengths,
    adapter_in,
    adapter_out,
    moment_in,
    square_in,
    moment_out,
    square_out,
):
    tok = queries.shape[1]
    width = out_grad.shape[2]
    rank = adapter_in.shape[1]
    groups = lax.axis_size("sp")
    chips = groups // 2
    reps = lax.axis_size("rep")
    ny = 4 if reps % 4 == 0 and reps > 4 else 1
    nz = reps // ny
    tokens = tok * groups
    depth = rank // groups
    in_lines, out_lines = HD // nz, (width // nz // HD) * depth
    bf16, f32 = jnp.bfloat16, jnp.float32
    vmem = pl.BlockSpec(memory_space=pltpu.VMEM)
    smem = pl.BlockSpec(memory_space=pltpu.SMEM)
    hbm = pl.BlockSpec(memory_space=pl.ANY)
    dma = pltpu.SemaphoreType.DMA

    def sum_bufs(first, lines):
        return [
            pltpu.VMEM((nz, first, HD), f32),
            pltpu.VMEM((nz, first, HD), f32),
            pltpu.VMEM((lines, HD), f32),
            pltpu.VMEM((ny, lines, HD), f32),
            pltpu.VMEM((lines, HD), f32),
            pltpu.VMEM((nz, lines, HD), f32),
        ]

    sum_sems = [dma((n,)) for n in (nz, nz, ny, ny, nz, nz)]
    grad_in, grad_out = pl.pallas_call(
        functools.partial(step_kernel, (tok, groups, nz, ny)),
        name="adapter_step",
        out_shape=(
            jax.ShapeDtypeStruct((HD, rank), f32),
            jax.ShapeDtypeStruct((depth, width), f32),
        ),
        in_specs=[smem, smem, hbm, hbm, hbm, hbm, hbm, hbm],
        out_specs=(vmem, vmem),
        scratch_shapes=[
            pltpu.VMEM((tokens, 2 * HD), bf16),
            pltpu.VMEM((tokens, 2 * HD), bf16),
            pltpu.VMEM((tokens, HD), bf16),
            pltpu.VMEM((2, 2 * tok, tokens), f32),
            pltpu.VMEM((2, 2 * tok, HD), f32),
            pltpu.VMEM((tokens, HD), bf16),
            pltpu.VMEM((tok, groups * HD), bf16),
            pltpu.VMEM((2, tok, width), bf16),
            pltpu.VMEM((HD, rank), f32),
            pltpu.VMEM((depth, width), f32),
            pltpu.VMEM((HD, rank), bf16),
            pltpu.VMEM((depth, width), bf16),
            pltpu.VMEM((groups, HD, rank), bf16),
            pltpu.VMEM((groups, depth, width), bf16),
            pltpu.VMEM((tokens, rank), bf16),
            pltpu.VMEM((2, tok, rank), bf16),
            pltpu.VMEM((chips, depth, width - nz * HD), f32),
            pltpu.VMEM((chips, depth, width - nz * HD), f32),
            pltpu.VMEM((nz, chips, depth, HD), f32),
            pltpu.VMEM((nz, chips, depth, HD), f32),
            pltpu.VMEM((chips, depth, HD), f32),
            pltpu.VMEM((chips, depth, HD), f32),
            sum_bufs(in_lines, in_lines),
            sum_bufs(out_lines - depth, out_lines),
            dma((3,)),
        ]
        + [dma(())] * 4
        + [dma((groups,))] * 14
        + [dma((chips,))] * 4
        + [dma((nz,))] * 6
        + [dma((2,))] * 2
        + [sum_sems, sum_sems],
        compiler_params=pltpu.CompilerParams(
            collective_id=0, has_side_effects=True, vmem_limit_bytes=60 * 2**20
        ),
    )(
        clip_count,
        clip_lengths,
        queries,
        key_rows,
        values,
        out_grad,
        adapter_in,
        adapter_out,
    )
    return tuple(
        pl.pallas_call(
            adamw_kernel,
            name="adamw",
            out_shape=[jax.ShapeDtypeStruct(a.shape, f32) for a in [grad_in] * 3 + [grad_out] * 3],
            in_specs=[vmem] * 8,
            out_specs=[vmem] * 6,
        )(
            adapter_in,
            grad_in,
            moment_in,
            square_in,
            adapter_out,
            grad_out,
            moment_out,
            square_out,
        )
    )


def solution(mesh):
    placed = (
        P("rep", "sp", None),
        P("rep", "sp", None),
        P("rep", "sp", None),
        P("rep", "sp", None),
        P("rep"),
        P("rep", None),
        P("sp", None),
        P("sp", None),
        P("sp", None),
        P("sp", None),
        P("sp", None),
        P("sp", None),
    )
    return jax.shard_map(
        per_device,
        mesh=mesh,
        in_specs=placed,
        out_specs=(
            P("sp", None),
            P("sp", None),
            P("sp", None),
            P("sp", None),
            P("sp", None),
            P("sp", None),
        ),
        check_vma=False,
    )
```

```python
import functools
import math

import jax
import jax.numpy as jnp
from jax import lax
from jax.experimental import pallas as pl
from jax.experimental.pallas import tpu as pltpu
from jax.sharding import PartitionSpec as P

HD = 128
MAX_CLIPS = 3
MESH = pl.DeviceIdType.MESH

first_rate = 0.9
second_rate = 0.999
adam_steps = 100.0
adam_epsilon = 1e-08
decay_rate = 0.1

EXP2_SCALE = HD ** (-0.5) * math.log2(math.e)
MASK = -131072.0
KEY_CHUNKS = 4
EARLY_CHIPS = 5
MORE = 3
ROWS = 64


def adamw(param, grad, moment, square):
    momentum = first_rate * moment + (1.0 - first_rate) * grad
    variance = second_rate * square + (1.0 - second_rate) * grad * grad
    first_hat = momentum / (1.0 - first_rate**adam_steps)
    second_hat = variance / (1.0 - second_rate**adam_steps)
    update = first_hat / (jnp.sqrt(second_hat) + adam_epsilon) + decay_rate * param
    return (momentum, variance, update)


def remote(src, dst, send_sem, recv_sem, device):
    return pltpu.make_async_remote_copy(
        src_ref=src,
        dst_ref=dst,
        send_sem=send_sem,
        recv_sem=recv_sem,
        device_id=device,
        device_id_type=MESH,
    )


def drain(ref, sem):
    pltpu.make_async_copy(ref, ref, sem).wait()


def each(n, body, start=0):
    def step(i, carry):
        body(i)
        return carry

    lax.fori_loop(start, n, step, 0)


def step_kernel(
    dims,
    count_ref,
    lengths_ref,
    q_hbm,
    k_hbm,
    v_hbm,
    og_hbm,
    ain_hbm,
    aout_hbm,
    gin_ref,
    gout_ref,
    q_all,
    k_all,
    v_all,
    scores_buf,
    high_buf,
    weights,
    totals,
    mixed,
    attended,
    og_all,
    ain_own,
    aout_own,
    ain_cast,
    aout_cast,
    ain_all,
    aout_all,
    slopes_all,
    adapted_all,
    summed,
    chip_in,
    z_first,
    z_first_in,
    tiles,
    tile_in,
    in_bufs,
    out_bufs,
    load_sems,
    og_s,
    og_r,
    ad_s,
    ad_r,
    k_s,
    k_r,
    v_s,
    v_r,
    q_s,
    q_r,
    o_s,
    o_r,
    ai_s,
    ai_r,
    ao_s,
    ao_r,
    sl_s,
    sl_r,
    pass_s,
    pass_r,
    chip_s,
    chip_r,
    ti_s,
    ti_r,
    zf_s,
    zf_r,
    az_s,
    az_r,
    cz_s,
    cz_r,
    half_s,
    half_r,
    in_sems,
    out_sems,
):
    tok, groups, nz, ny = dims
    chips = groups // 2
    tokens = tok * groups
    rank = ain_hbm.shape[1]
    inner = HD * groups
    me = lax.axis_index("sp")
    rep = lax.axis_index("rep")
    chip = me // 2
    core = lax.rem(me, 2)
    partner = me + 1 - 2 * core
    z = rep // ny
    y = lax.rem(rep, ny)

    def rows(s):
        return pl.ds(pl.multiple_of(s * tok, tok), tok)

    def lanes(s):
        return pl.ds(pl.multiple_of(s * HD, HD), HD)

    def same_core(i):
        return 2 * lax.rem(chip + i, chips) + core

    barrier = pltpu.get_barrier_semaphore()

    def greet_sp(i):
        pl.semaphore_signal(
            barrier, inc=1, device_id={"sp": lax.rem(me + i, groups)}, device_id_type=MESH
        )

    def greet_z(i):
        pl.semaphore_signal(
            barrier,
            inc=1,
            device_id={"rep": lax.rem(z + i, nz) * ny + y},
            device_id_type=MESH,
        )

    def greet_y(i):
        pl.semaphore_signal(
            barrier,
            inc=1,
            device_id={"rep": z * ny + lax.rem(y + i, ny)},
            device_id_type=MESH,
        )

    each(groups, greet_sp, 1)
    each(nz, greet_z, 1)
    each(ny, greet_y, 1)

    load_og = pltpu.make_async_copy(og_hbm.at[0], og_all.at[core], load_sems.at[0])
    load_ain = pltpu.make_async_copy(ain_hbm, ain_own, load_sems.at[1])
    load_aout = pltpu.make_async_copy(aout_hbm, aout_own, load_sems.at[2])
    load_ain.start()
    load_aout.start()
    load_og.start()
    pl.semaphore_wait(barrier, groups + nz + ny - 3)

    def head_to(src, dst, s, r, device):
        return remote(
            src.at[0, :, lanes(device)],
            dst.at[rows(me), pl.ds(0, HD)],
            s,
            r,
            {"sp": device},
        )

    def own_head(src, dst, r):
        return pltpu.make_async_copy(
            src.at[0, :, lanes(me)], dst.at[rows(me), pl.ds(0, HD)], r
        )

    def to_peer(i):
        return lax.rem(me - i + groups, groups)


    half = groups // 2
    in_rows = HD // nz
    out_cols = gout_ref.shape[1] // nz
    side = me // half
    z_cols = pl.ds(pl.multiple_of(z * out_cols, out_cols), out_cols)
    z_rows = pl.ds(pl.multiple_of(z * in_rows, in_rows), in_rows)

    def share_device(i):
        return 2 * lax.rem(chip + i, chips) + side

    def aout_share(device):
        return remote(
            aout_cast.at[:, z_cols],
            aout_all.at[me, :, z_cols],
            ao_s,
            ao_r,
            {"sp": device},
        )

    def ain_share(device):
        return remote(
            ain_cast.at[z_rows], ain_all.at[me, z_rows], ai_s, ai_r, {"sp": device}
        )

    load_ain.wait()
    load_aout.wait()
    ain_cast[...] = ain_own[...].astype(jnp.bfloat16)
    aout_cast[...] = aout_own[...].astype(jnp.bfloat16)

    @pl.when(core == side)
    def _():
        pltpu.make_async_copy(
            aout_cast.at[:, z_cols], aout_all.at[me, :, z_cols], ao_r
        ).start()
        pltpu.make_async_copy(ain_cast.at[z_rows], ain_all.at[me, z_rows], ai_r).start()

    @pl.when(core != side)
    def _():
        aout_share(partner).start()
        ain_share(partner).start()

    def send_share(i):
        aout_share(share_device(i)).start()
        ain_share(share_device(i)).start()

    each(chips, send_share, 1)

    def to_chip(src, dst, send, recv, j):
        for c in range(2):
            head_to(src, dst, send, recv, 2 * lax.rem(chip - j + chips, chips) + c).start()

    def queries_to(j):
        to_chip(q_hbm, q_all, q_s, q_r.at[chip], j)

    def values_to(j):
        to_chip(v_hbm, v_all, v_s, v_r, j)

    own_head(k_hbm, k_all, k_r).start()
    each(groups, lambda i: head_to(k_hbm, k_all, k_s, k_r, to_peer(i)).start(), 1)
    own_head(q_hbm, q_all, q_r.at[chip]).start()
    own_head(v_hbm, v_all, v_r).start()
    head_to(q_hbm, q_all, q_s, q_r.at[chip], partner).start()
    head_to(v_hbm, v_all, v_s, v_r, partner).start()
    queries_to(1)

    send_og = remote(og_hbm.at[0], og_all.at[core], og_s, og_r, {"sp": partner})
    send_og.start()

    ends = []
    for j in range(MAX_CLIPS):
        length = jnp.where(count_ref[0] > j, lengths_ref[0, j], 0)
        ends.append(length if j == 0 else ends[-1] + length)

    def segment(positions):
        return sum((positions >= e).astype(jnp.int32) for e in ends)

    block = 2 * tok

    def features(b):
        r = pl.ds(pl.multiple_of(b * block, block), block)
        at = b * block + lax.broadcasted_iota(jnp.int32, (block, HD), 0)
        feature = lax.broadcasted_iota(jnp.int32, (block, HD), 1)
        seg = segment(at)
        same = seg == feature
        k_all[r, HD:] = jnp.where(same, 1.0, 0.0).astype(jnp.bfloat16)
        other = jnp.where(feature <= MAX_CLIPS, MASK, 0.0)
        q_all[r, HD:] = jnp.where(same, 0.0, other).astype(jnp.bfloat16)

    each(chips, features)
    mine = me * tok + lax.broadcasted_iota(jnp.int32, (tok, rank), 0)
    live = segment(mine) < MAX_CLIPS

    owners = pl.ds(pl.multiple_of(core * half, half), half)

    drain(aout_all.at[owners, :, z_cols], ao_r)
    drain(ain_all.at[owners, z_rows], ai_r)

    def z_peer(i):
        return lax.rem(z + i, nz)

    def aout_along(p, origin):
        cols = pl.ds(pl.multiple_of(origin * out_cols, out_cols), out_cols)
        part = aout_all.at[owners, :, cols]
        return remote(part, part, az_s, az_r, {"rep": p * ny + y})

    def ain_along(p, origin):
        lines = pl.ds(pl.multiple_of(origin * in_rows, in_rows), in_rows)
        part = ain_all.at[owners, lines]
        return remote(part, part, cz_s, cz_r, {"rep": p * ny + y})

    def send_along(i):
        aout_along(z_peer(i), z).start()
        ain_along(z_peer(i), z).start()

    each(nz, send_along, 1)

    others = aout_all.at[owners, :, pl.ds(0, (nz - 1) * out_cols)]
    other_lines = ain_all.at[owners, pl.ds(0, (nz - 1) * in_rows)]

    swap_out = remote(
        aout_all.at[owners], aout_all.at[owners], half_s.at[0], half_r.at[0], {"sp": partner}
    )
    swap_in = remote(
        ain_all.at[owners], ain_all.at[owners], half_s.at[1], half_r.at[1], {"sp": partner}
    )

    def slopes_to(owner, device, s, r):
        part = slopes_all.at[rows(owner)]
        return remote(part, part, s, r, {"sp": device})

    def change_cores():
        drain(others, az_r)
        drain(other_lines, cz_r)
        swap_out.start()
        swap_in.start()

    def make_slopes():
        swap_out.wait_recv()
        swap_in.wait_recv()
        load_og.wait()
        outer = jnp.concatenate([aout_all[i].astype(jnp.float32) for i in range(groups)], axis=0)
        slopes = lax.dot_general(
            og_all[core],
            outer.astype(jnp.bfloat16),
            (((1,), (1,)), ((), ())),
            preferred_element_type=jnp.float32,
        ) * rank ** (-0.5)
        slopes_all[rows(me)] = jnp.where(live, slopes, 0.0).astype(jnp.bfloat16)

    def spread_slopes():
        slopes_to(me, partner, sl_s, pass_r).start()
        each(chips, lambda i: slopes_to(me, same_core(i), sl_s, sl_r).start(), 1)

    drain(k_all.at[pl.ds(0, tokens - tok), pl.ds(0, HD)], k_s)
    each(EARLY_CHIPS, queries_to, 2)

    def send_more(n):
        pl.when(n < chips - EARLY_CHIPS)(lambda: queries_to(EARLY_CHIPS + n))
        j = n - (chips - EARLY_CHIPS) + 1
        pl.when((j >= 1) & (j < chips))(lambda: values_to(j))

    drain(k_all.at[:, pl.ds(0, HD)], k_r)

    def chip_of(i):
        return lax.rem(chip + i, chips)

    def block_rows(i):
        return pl.ds(pl.multiple_of(chip_of(i) * block, block), block)

    def wait_queries(i):
        drain(q_all.at[block_rows(i), pl.ds(0, HD)], q_r.at[chip_of(i)])

    width = tokens // KEY_CHUNKS

    def scores(i, slot):
        query = q_all[block_rows(i), :]
        high = None
        for c in range(KEY_CHUNKS):
            s = lax.dot_general(
                query,
                k_all[c * width : (c + 1) * width, :],
                (((1,), (1,)), ((), ())),
                preferred_element_type=jnp.float32,
            )
            scores_buf[slot, :, c * width : (c + 1) * width] = s
            for j in range(width // HD):
                piece = s[:, j * HD : (j + 1) * HD]
                high = piece if high is None else jnp.maximum(high, piece)
        high_buf[slot] = jnp.broadcast_to(jnp.max(high, axis=1, keepdims=True), (block, HD))

    def weigh(i, slot):
        at = pl.multiple_of(chip_of(i) * block, block)
        for g in range(block // ROWS):
            lines = slice(g * ROWS, (g + 1) * ROWS)
            high = high_buf[slot, lines]
            row_total = None
            for j in range(tokens // HD):
                s = scores_buf[slot, lines, j * HD : (j + 1) * HD]
                exponent = jnp.exp2((s - high) * EXP2_SCALE)
                row_total = exponent if row_total is None else row_total + exponent
                weights[pl.ds(at + g * ROWS, ROWS), j * HD : (j + 1) * HD] = exponent.astype(
                    jnp.bfloat16
                )
            totals[pl.ds(at + g * ROWS, ROWS), :] = jnp.broadcast_to(
                jnp.sum(row_total, axis=1, keepdims=True), (ROWS, HD)
            )

    def mix(i):
        product = jnp.dot(
            weights[block_rows(i), :], v_all[...], preferred_element_type=jnp.float32
        )
        mixed[block_rows(i), :] = (product / totals[block_rows(i), :]).astype(jnp.bfloat16)

    def mixed_to(device):
        return remote(
            mixed.at[rows(device)],
            attended.at[:, lanes(me)],
            o_s,
            o_r,
            {"sp": device},
        )

    def own_mixed():
        return pltpu.make_async_copy(mixed.at[rows(me)], attended.at[:, lanes(me)], o_r)

    def give_back(i):
        for c in range(2):
            device = 2 * chip_of(i) + c

            @pl.when(device == me)
            def _():
                own_mixed().start()

            @pl.when(device != me)
            def _():
                mixed_to(device).start()

    wait_queries(0)
    scores(0, 0)

    def two_blocks(t):
        i = 2 * t
        each(MORE, lambda n: send_more(MORE * i + n))
        wait_queries(i + 1)
        scores(i + 1, 1)
        weigh(i, 0)
        each(MORE, lambda n: send_more(MORE * i + MORE + n))
        wait_queries(i + 2)
        scores(i + 2, 0)
        weigh(i + 1, 1)

    each(chips // 2 - 1, two_blocks)
    wait_queries(chips - 1)
    scores(chips - 1, 1)
    weigh(chips - 2, 0)
    change_cores()
    weigh(chips - 1, 1)
    make_slopes()
    drain(v_all, v_r)

    def mix_block(n):
        i = lax.rem(n + 1, chips)
        mix(i)
        give_back(i)

    each(chips, mix_block)
    drain(mixed.at[pl.ds(0, tokens - tok)], o_s)
    spread_slopes()

    out_tiles = out_cols // HD

    def y_peer(i):
        return lax.rem(y + i, ny)

    class Replicas:
        def __init__(self, bufs, sems):
            self.pack, self.z_in, self.y_out, self.y_in, self.z_out, self.whole = bufs
            self.zi_s, self.zi_r, self.y_s, self.y_r, self.zo_s, self.zo_r = sems

        def z_copy(self, p, origin):
            return remote(
                self.pack.at[p],
                self.z_in.at[origin],
                self.zi_s,
                self.zi_r,
                {"rep": p * ny + y},
            )

        def y_copy(self, p, origin):
            return remote(
                self.y_out,
                self.y_in.at[origin],
                self.y_s,
                self.y_r,
                {"rep": z * ny + p},
            )

        def back_copy(self, p, origin):
            return remote(
                self.z_out,
                self.whole.at[origin],
                self.zo_s,
                self.zo_r,
                {"rep": p * ny + y},
            )

        def start(self):
            each(nz, lambda i: self.z_copy(z_peer(i), z).start(), 1)
            self.z_in[z] = self.pack[z]

        def across(self, more=None):
            drain(self.z_in.at[pl.ds(0, nz - 1)], self.zi_r)
            total = self.z_in[0]
            for p in range(1, nz):
                total = total + self.z_in[p]
            if more is not None:
                total = jnp.concatenate([total, more], axis=0)
            self.y_out[...] = total
            each(ny, lambda i: self.y_copy(y_peer(i), y).start(), 1)
            self.y_in[y] = total

        def back(self):
            drain(self.y_in.at[pl.ds(0, ny - 1)], self.y_r)
            total = self.y_in[0]
            for p in range(1, ny):
                total = total + self.y_in[p]
            self.z_out[...] = total
            each(nz, lambda i: self.back_copy(z_peer(i), z).start(), 1)
            self.whole[z] = total

        def arrive(self):
            drain(self.whole.at[pl.ds(0, nz - 1)], self.zo_r)

        def sent(self):
            drain(self.pack.at[pl.ds(0, nz - 1)], self.zi_s)
            drain(self.y_in.at[pl.ds(0, ny - 1)], self.y_s)
            drain(self.whole.at[pl.ds(0, nz - 1)], self.zo_s)

    drain(attended, o_r)
    adapted = jnp.dot(
        attended[...], ain_all[...].reshape(inner, rank), preferred_element_type=jnp.float32
    )
    adapted_all[core] = jnp.where(live, adapted * inner ** (-0.5), 0.0).astype(jnp.bfloat16)
    send_adapted = remote(adapted_all.at[core], adapted_all.at[core], ad_s, ad_r, {"sp": partner})
    send_adapted.start()
    send_og.wait_recv()
    send_adapted.wait_recv()
    term_out = lax.dot_general(
        adapted_all[...].reshape(block, rank),
        og_all[...].reshape(block, og_all.shape[2]),
        (((0,), (0,)), ((), ())),
        preferred_element_type=jnp.float32,
    ) * rank ** (-0.5)
    depth = rank // groups

    chip_tiles = out_tiles - 1
    chip_cols = chip_tiles * HD * nz
    for j in range(chips):
        at = 2 * j * depth
        own = jnp.where(
            core == 0, term_out[at : at + depth], term_out[at + depth : at + 2 * depth]
        )
        summed[j] = own[:, :chip_cols]
        for p in range(nz):
            z_first[p, j] = own[:, chip_cols + p * HD : chip_cols + (p + 1) * HD]

    def chunk_to(j, origin):
        return remote(
            summed.at[j],
            chip_in.at[origin],
            chip_s,
            chip_r,
            {"sp": 2 * j + core},
        )

    def z_first_to(p, origin):
        return remote(
            z_first.at[p],
            z_first_in.at[origin],
            zf_s,
            zf_r,
            {"rep": p * ny + y},
        )

    def tile_to(j, origin):
        return remote(
            tiles.at[j], tile_in.at[origin], ti_s, ti_r, {"sp": 2 * j + core}
        )

    each(chips, lambda i: chunk_to(chip_of(i), chip).start(), 1)
    each(nz, lambda i: z_first_to(z_peer(i), z).start(), 1)
    chip_in[chip] = summed[chip]
    z_first_in[z] = z_first[z]

    drain(slopes_all.at[pl.ds(0, (chips - 1) * tok)], sl_r)
    each(chips, lambda i: slopes_to(same_core(i), partner, pass_s, pass_r).start(), 1)

    drain(z_first_in.at[pl.ds(0, nz - 1)], zf_r)
    own = z_first_in[0]
    for p in range(1, nz):
        own = own + z_first_in[p]
    tiles[...] = own
    each(chips, lambda i: tile_to(chip_of(i), chip).start(), 1)
    tile_in[chip] = tiles[chip]

    drain(slopes_all.at[pl.ds(0, chips * tok)], pass_r)
    grad_in = lax.dot_general(
        mixed[...], slopes_all[...], (((0,), (0,)), ((), ())), preferred_element_type=jnp.float32
    ) * inner ** (-0.5)
    sum_in = Replicas(in_bufs, in_sems)
    sum_out = Replicas(out_bufs, out_sems)
    for p in range(nz):
        sum_in.pack[p] = grad_in[p * in_rows : (p + 1) * in_rows]
    sum_in.start()

    drain(chip_in.at[pl.ds(0, chips - 1)], chip_r)
    own = chip_in[0]
    for j in range(1, chips):
        own = own + chip_in[j]
    for p in range(nz):
        for t in range(chip_tiles):
            at = (p * chip_tiles + t) * HD
            sum_out.pack[p, t * depth : (t + 1) * depth] = own[:, at : at + HD]
    sum_out.start()
    sum_in.across()
    drain(tile_in.at[pl.ds(0, chips - 1)], ti_r)
    own = tile_in[0]
    for j in range(1, chips):
        own = own + tile_in[j]
    sum_out.across(own)
    sum_in.back()
    sum_out.back()
    sum_in.arrive()
    for p in range(nz):
        gin_ref[p * in_rows : (p + 1) * in_rows] = sum_in.whole[p]

    @pl.when(core != side)
    def _():
        drain(aout_all.at[pl.ds(0, chips), :, z_cols], ao_s)
        drain(ain_all.at[pl.ds(0, chips), z_rows], ai_s)

    @pl.when(core == side)
    def _():
        drain(aout_all.at[pl.ds(0, chips - 1), :, z_cols], ao_s)
        drain(ain_all.at[pl.ds(0, chips - 1), z_rows], ai_s)

    drain(q_all.at[pl.ds(0, tokens - tok), pl.ds(0, HD)], q_s)
    drain(v_all.at[pl.ds(0, tokens - tok)], v_s)
    drain(others, az_s)
    drain(other_lines, cz_s)
    drain(slopes_all.at[pl.ds(0, chips * tok)], sl_s)
    drain(slopes_all.at[pl.ds(0, (chips - 1) * tok)], pass_s)
    drain(chip_in.at[pl.ds(0, chips - 1)], chip_s)
    drain(tile_in.at[pl.ds(0, chips - 1)], ti_s)
    drain(z_first_in.at[pl.ds(0, nz - 1)], zf_s)
    send_og.wait_send()
    send_adapted.wait_send()
    swap_out.wait_send()
    swap_in.wait_send()
    sum_in.sent()
    sum_out.sent()
    sum_out.arrive()
    for p in range(nz):
        for t in range(chip_tiles):
            at = (p * chip_tiles + t) * HD
            gout_ref[:, at : at + HD] = sum_out.whole[p, t * depth : (t + 1) * depth]
        at = chip_cols + p * HD
        gout_ref[:, at : at + HD] = sum_out.whole[p, chip_tiles * depth :]


def adamw_kernel(*refs):
    ins, outs = refs[:8], refs[8:]
    for at in range(2):
        param, grad, moment, square = (r[...] for r in ins[4 * at : 4 * at + 4])
        for ref, value in zip(outs[3 * at : 3 * at + 3], adamw(param, grad, moment, square)):
            ref[...] = value


def per_device(
    queries,
    key_rows,
    values,
    out_grad,
    clip_count,
    clip_lengths,
    adapter_in,
    adapter_out,
    moment_in,
    square_in,
    moment_out,
    square_out,
):
    tok = queries.shape[1]
    width = out_grad.shape[2]
    rank = adapter_in.shape[1]
    groups = lax.axis_size("sp")
    chips = groups // 2
    reps = lax.axis_size("rep")
    ny = 4 if reps % 4 == 0 and reps > 4 else 1
    nz = reps // ny
    tokens = tok * groups
    depth = rank // groups
    in_lines, out_lines = HD // nz, (width // nz // HD) * depth
    bf16, f32 = jnp.bfloat16, jnp.float32
    vmem = pl.BlockSpec(memory_space=pltpu.VMEM)
    smem = pl.BlockSpec(memory_space=pltpu.SMEM)
    hbm = pl.BlockSpec(memory_space=pl.ANY)
    dma = pltpu.SemaphoreType.DMA

    def sum_bufs(first, lines):
        return [
            pltpu.VMEM((nz, first, HD), f32),
            pltpu.VMEM((nz, first, HD), f32),
            pltpu.VMEM((lines, HD), f32),
            pltpu.VMEM((ny, lines, HD), f32),
            pltpu.VMEM((lines, HD), f32),
            pltpu.VMEM((nz, lines, HD), f32),
        ]

    sum_sems = [dma(())] * 6
    grad_in, grad_out = pl.pallas_call(
        functools.partial(step_kernel, (tok, groups, nz, ny)),
        name="adapter_step",
        out_shape=(
            jax.ShapeDtypeStruct((HD, rank), f32),
            jax.ShapeDtypeStruct((depth, width), f32),
        ),
        in_specs=[smem, smem, hbm, hbm, hbm, hbm, hbm, hbm],
        out_specs=(vmem, vmem),
        scratch_shapes=[
            pltpu.VMEM((tokens, 2 * HD), bf16),
            pltpu.VMEM((tokens, 2 * HD), bf16),
            pltpu.VMEM((tokens, HD), bf16),
            pltpu.VMEM((2, 2 * tok, tokens), f32),
            pltpu.VMEM((2, 2 * tok, HD), f32),
            pltpu.VMEM((tokens, tokens), bf16),
            pltpu.VMEM((tokens, HD), f32),
            pltpu.VMEM((tokens, HD), bf16),
            pltpu.VMEM((tok, groups * HD), bf16),
            pltpu.VMEM((2, tok, width), bf16),
            pltpu.VMEM((HD, rank), f32),
            pltpu.VMEM((depth, width), f32),
            pltpu.VMEM((HD, rank), bf16),
            pltpu.VMEM((depth, width), bf16),
            pltpu.VMEM((groups, HD, rank), bf16),
            pltpu.VMEM((groups, depth, width), bf16),
            pltpu.VMEM((tokens, rank), bf16),
            pltpu.VMEM((2, tok, rank), bf16),
            pltpu.VMEM((chips, depth, width - nz * HD), f32),
            pltpu.VMEM((chips, depth, width - nz * HD), f32),
            pltpu.VMEM((nz, chips, depth, HD), f32),
            pltpu.VMEM((nz, chips, depth, HD), f32),
            pltpu.VMEM((chips, depth, HD), f32),
            pltpu.VMEM((chips, depth, HD), f32),
            sum_bufs(in_lines, in_lines),
            sum_bufs(out_lines - depth, out_lines),
            dma((3,)),
        ]
        + [dma(())] * 9
        + [dma((chips,))]
        + [dma(())] * 20
        + [dma((2,))] * 2
        + [sum_sems, sum_sems],
        compiler_params=pltpu.CompilerParams(
            collective_id=0, has_side_effects=True, vmem_limit_bytes=60 * 2**20
        ),
    )(
        clip_count,
        clip_lengths,
        queries,
        key_rows,
        values,
        out_grad,
        adapter_in,
        adapter_out,
    )
    return tuple(
        pl.pallas_call(
            adamw_kernel,
            name="adamw",
            out_shape=[jax.ShapeDtypeStruct(a.shape, f32) for a in [grad_in] * 3 + [grad_out] * 3],
            in_specs=[vmem] * 8,
            out_specs=[vmem] * 6,
        )(
            adapter_in,
            grad_in,
            moment_in,
            square_in,
            adapter_out,
            grad_out,
            moment_out,
            square_out,
        )
    )


def solution(mesh):
    placed = (
        P("rep", "sp", None),
        P("rep", "sp", None),
        P("rep", "sp", None),
        P("rep", "sp", None),
        P("rep"),
        P("rep", None),
        P("sp", None),
        P("sp", None),
        P("sp", None),
        P("sp", None),
        P("sp", None),
        P("sp", None),
    )
    return jax.shard_map(
        per_device,
        mesh=mesh,
        in_specs=placed,
        out_specs=(
            P("sp", None),
            P("sp", None),
            P("sp", None),
            P("sp", None),
            P("sp", None),
            P("sp", None),
        ),
        check_vma=False,
    )
```

```python
import functools
import math

import jax
import jax.numpy as jnp
from jax import lax
from jax.experimental import pallas as pl
from jax.experimental.pallas import tpu as pltpu
from jax.sharding import PartitionSpec as P

HD = 128
MAX_CLIPS = 3
MESH = pl.DeviceIdType.MESH

first_rate = 0.9
second_rate = 0.999
adam_steps = 100.0
adam_epsilon = 1e-08
decay_rate = 0.1

EXP2_SCALE = HD ** (-0.5) * math.log2(math.e)
MASK = -131072.0
KEY_CHUNKS = 4
EARLY_CHIPS = 5
MORE = 3
ROWS = 64


def adamw(param, grad, moment, square):
    momentum = first_rate * moment + (1.0 - first_rate) * grad
    variance = second_rate * square + (1.0 - second_rate) * grad * grad
    first_hat = momentum / (1.0 - first_rate**adam_steps)
    second_hat = variance / (1.0 - second_rate**adam_steps)
    update = first_hat / (jnp.sqrt(second_hat) + adam_epsilon) + decay_rate * param
    return (momentum, variance, update)


def remote(src, dst, send_sem, recv_sem, device):
    return pltpu.make_async_remote_copy(
        src_ref=src,
        dst_ref=dst,
        send_sem=send_sem,
        recv_sem=recv_sem,
        device_id=device,
        device_id_type=MESH,
    )


def drain(ref, sem):
    pltpu.make_async_copy(ref, ref, sem).wait()


def each(n, body, start=0):
    def step(i, carry):
        body(i)
        return carry

    lax.fori_loop(start, n, step, 0)


def step_kernel(
    dims,
    count_ref,
    lengths_ref,
    q_hbm,
    k_hbm,
    v_hbm,
    og_hbm,
    ain_hbm,
    aout_hbm,
    gin_ref,
    gout_ref,
    q_all,
    k_all,
    v_all,
    scores_buf,
    high_buf,
    weights,
    totals,
    mixed,
    attended,
    og_all,
    ain_own,
    aout_own,
    ain_cast,
    aout_cast,
    ain_all,
    aout_all,
    slopes_all,
    adapted_all,
    summed,
    chip_in,
    z_first,
    z_first_in,
    tiles,
    tile_in,
    in_bufs,
    out_bufs,
    load_sems,
    og_s,
    og_r,
    ad_s,
    ad_r,
    k_s,
    k_r,
    v_s,
    v_r,
    q_s,
    q_r,
    o_s,
    o_r,
    ai_s,
    ai_r,
    ao_s,
    ao_r,
    sl_s,
    sl_r,
    pass_s,
    pass_r,
    chip_s,
    chip_r,
    ti_s,
    ti_r,
    zf_s,
    zf_r,
    az_s,
    az_r,
    cz_s,
    cz_r,
    half_s,
    half_r,
    in_sems,
    out_sems,
):
    tok, groups, nz, ny = dims
    chips = groups // 2
    tokens = tok * groups
    rank = ain_hbm.shape[1]
    inner = HD * groups
    me = lax.axis_index("sp")
    rep = lax.axis_index("rep")
    chip = me // 2
    core = lax.rem(me, 2)
    partner = me + 1 - 2 * core
    z = rep // ny
    y = lax.rem(rep, ny)

    def rows(s):
        return pl.ds(pl.multiple_of(s * tok, tok), tok)

    def lanes(s):
        return pl.ds(pl.multiple_of(s * HD, HD), HD)

    def same_core(i):
        return 2 * lax.rem(chip + i, chips) + core

    barrier = pltpu.get_barrier_semaphore()

    def greet_sp(i):
        pl.semaphore_signal(
            barrier, inc=1, device_id={"sp": lax.rem(me + i, groups)}, device_id_type=MESH
        )

    def greet_z(i):
        pl.semaphore_signal(
            barrier,
            inc=1,
            device_id={"rep": lax.rem(z + i, nz) * ny + y},
            device_id_type=MESH,
        )

    def greet_y(i):
        pl.semaphore_signal(
            barrier,
            inc=1,
            device_id={"rep": z * ny + lax.rem(y + i, ny)},
            device_id_type=MESH,
        )

    each(groups, greet_sp, 1)
    each(nz, greet_z, 1)
    each(ny, greet_y, 1)

    load_og = pltpu.make_async_copy(og_hbm.at[0], og_all.at[core], load_sems.at[0])
    load_ain = pltpu.make_async_copy(ain_hbm, ain_own, load_sems.at[1])
    load_aout = pltpu.make_async_copy(aout_hbm, aout_own, load_sems.at[2])
    load_ain.start()
    load_aout.start()
    load_og.start()
    pl.semaphore_wait(barrier, groups + nz + ny - 3)

    def head_to(src, dst, s, r, device):
        return remote(
            src.at[0, :, lanes(device)],
            dst.at[rows(me), pl.ds(0, HD)],
            s,
            r,
            {"sp": device},
        )

    def own_head(src, dst, r):
        return pltpu.make_async_copy(
            src.at[0, :, lanes(me)], dst.at[rows(me), pl.ds(0, HD)], r
        )

    def to_peer(i):
        return lax.rem(me - i + groups, groups)


    half = groups // 2
    in_rows = HD // nz
    out_cols = gout_ref.shape[1] // nz
    side = me // half
    z_cols = pl.ds(pl.multiple_of(z * out_cols, out_cols), out_cols)
    z_rows = pl.ds(pl.multiple_of(z * in_rows, in_rows), in_rows)

    def share_device(i):
        return 2 * lax.rem(chip + i, chips) + side

    def aout_share(device):
        return remote(
            aout_cast.at[:, z_cols],
            aout_all.at[me, :, z_cols],
            ao_s,
            ao_r,
            {"sp": device},
        )

    def ain_share(device):
        return remote(
            ain_cast.at[z_rows], ain_all.at[me, z_rows], ai_s, ai_r, {"sp": device}
        )

    load_ain.wait()
    load_aout.wait()
    ain_cast[...] = ain_own[...].astype(jnp.bfloat16)
    aout_cast[...] = aout_own[...].astype(jnp.bfloat16)

    @pl.when(core == side)
    def _():
        pltpu.make_async_copy(
            aout_cast.at[:, z_cols], aout_all.at[me, :, z_cols], ao_r
        ).start()
        pltpu.make_async_copy(ain_cast.at[z_rows], ain_all.at[me, z_rows], ai_r).start()

    @pl.when(core != side)
    def _():
        aout_share(partner).start()
        ain_share(partner).start()

    def send_share(i):
        aout_share(share_device(i)).start()
        ain_share(share_device(i)).start()

    each(chips, send_share, 1)

    def to_chip(src, dst, send, recv, j):
        for c in range(2):
            head_to(src, dst, send, recv, 2 * lax.rem(chip - j + chips, chips) + c).start()

    def queries_to(j):
        to_chip(q_hbm, q_all, q_s, q_r.at[chip], j)

    def values_to(j):
        to_chip(v_hbm, v_all, v_s, v_r, j)

    own_head(k_hbm, k_all, k_r).start()
    each(groups, lambda i: head_to(k_hbm, k_all, k_s, k_r, to_peer(i)).start(), 1)
    own_head(q_hbm, q_all, q_r.at[chip]).start()
    own_head(v_hbm, v_all, v_r).start()
    head_to(q_hbm, q_all, q_s, q_r.at[chip], partner).start()
    head_to(v_hbm, v_all, v_s, v_r, partner).start()
    queries_to(1)

    send_og = remote(og_hbm.at[0], og_all.at[core], og_s, og_r, {"sp": partner})
    send_og.start()

    ends = []
    for j in range(MAX_CLIPS):
        length = jnp.where(count_ref[0] > j, lengths_ref[0, j], 0)
        ends.append(length if j == 0 else ends[-1] + length)

    def segment(positions):
        return sum((positions >= e).astype(jnp.int32) for e in ends)

    block = 2 * tok

    def features(b):
        r = pl.ds(pl.multiple_of(b * block, block), block)
        at = b * block + lax.broadcasted_iota(jnp.int32, (block, HD), 0)
        feature = lax.broadcasted_iota(jnp.int32, (block, HD), 1)
        seg = segment(at)
        same = seg == feature
        k_all[r, HD:] = jnp.where(same, 1.0, 0.0).astype(jnp.bfloat16)
        other = jnp.where(feature <= MAX_CLIPS, MASK, 0.0)
        q_all[r, HD:] = jnp.where(same, 0.0, other).astype(jnp.bfloat16)

    each(chips, features)
    mine = me * tok + lax.broadcasted_iota(jnp.int32, (tok, rank), 0)
    live = segment(mine) < MAX_CLIPS

    owners = pl.ds(pl.multiple_of(core * half, half), half)

    drain(aout_all.at[owners, :, z_cols], ao_r)
    drain(ain_all.at[owners, z_rows], ai_r)

    def z_peer(i):
        return lax.rem(z + i, nz)

    def aout_along(p, origin):
        cols = pl.ds(pl.multiple_of(origin * out_cols, out_cols), out_cols)
        part = aout_all.at[owners, :, cols]
        return remote(part, part, az_s, az_r, {"rep": p * ny + y})

    def ain_along(p, origin):
        lines = pl.ds(pl.multiple_of(origin * in_rows, in_rows), in_rows)
        part = ain_all.at[owners, lines]
        return remote(part, part, cz_s, cz_r, {"rep": p * ny + y})

    def send_along(i):
        aout_along(z_peer(i), z).start()
        ain_along(z_peer(i), z).start()

    each(nz, send_along, 1)

    others = aout_all.at[owners, :, pl.ds(0, (nz - 1) * out_cols)]
    other_lines = ain_all.at[owners, pl.ds(0, (nz - 1) * in_rows)]

    swap_out = remote(
        aout_all.at[owners], aout_all.at[owners], half_s.at[0], half_r.at[0], {"sp": partner}
    )
    swap_in = remote(
        ain_all.at[owners], ain_all.at[owners], half_s.at[1], half_r.at[1], {"sp": partner}
    )

    def slopes_to(owner, device, s, r):
        part = slopes_all.at[rows(owner)]
        return remote(part, part, s, r, {"sp": device})

    def change_cores():
        drain(others, az_r)
        drain(other_lines, cz_r)
        swap_out.start()
        swap_in.start()

    def make_slopes():
        swap_out.wait_recv()
        swap_in.wait_recv()
        load_og.wait()
        outer = jnp.concatenate([aout_all[i].astype(jnp.float32) for i in range(groups)], axis=0)
        slopes = lax.dot_general(
            og_all[core],
            outer.astype(jnp.bfloat16),
            (((1,), (1,)), ((), ())),
            preferred_element_type=jnp.float32,
        ) * rank ** (-0.5)
        slopes_all[rows(me)] = jnp.where(live, slopes, 0.0).astype(jnp.bfloat16)

    def spread_slopes():
        slopes_to(me, partner, sl_s, pass_r).start()
        each(chips, lambda i: slopes_to(me, same_core(i), sl_s, sl_r).start(), 1)

    drain(k_all.at[pl.ds(0, tokens - tok), pl.ds(0, HD)], k_s)
    each(EARLY_CHIPS, queries_to, 2)

    def send_more(n):
        pl.when(n < chips - EARLY_CHIPS)(lambda: queries_to(EARLY_CHIPS + n))
        j = n - (chips - EARLY_CHIPS) + 1
        pl.when((j >= 1) & (j < chips))(lambda: values_to(j))

    drain(k_all.at[:, pl.ds(0, HD)], k_r)

    def chip_of(i):
        return lax.rem(chip + i, chips)

    def block_rows(i):
        return pl.ds(pl.multiple_of(chip_of(i) * block, block), block)

    def wait_queries(i):
        drain(q_all.at[block_rows(i), pl.ds(0, HD)], q_r.at[chip_of(i)])

    width = tokens // KEY_CHUNKS

    def scores(i, slot):
        query = q_all[block_rows(i), :]
        high = None
        for c in range(KEY_CHUNKS):
            s = lax.dot_general(
                query,
                k_all[c * width : (c + 1) * width, :],
                (((1,), (1,)), ((), ())),
                preferred_element_type=jnp.float32,
            )
            scores_buf[slot, :, c * width : (c + 1) * width] = s
            for j in range(width // HD):
                piece = s[:, j * HD : (j + 1) * HD]
                high = piece if high is None else jnp.maximum(high, piece)
        high_buf[slot] = jnp.broadcast_to(jnp.max(high, axis=1, keepdims=True), (block, HD))

    def weigh(i, slot):
        at = pl.multiple_of(chip_of(i) * block, block)
        for g in range(block // ROWS):
            lines = slice(g * ROWS, (g + 1) * ROWS)
            high = high_buf[slot, lines]
            row_total = None
            for j in range(tokens // HD):
                s = scores_buf[slot, lines, j * HD : (j + 1) * HD]
                exponent = jnp.exp2((s - high) * EXP2_SCALE)
                row_total = exponent if row_total is None else row_total + exponent
                weights[pl.ds(at + g * ROWS, ROWS), j * HD : (j + 1) * HD] = exponent.astype(
                    jnp.bfloat16
                )
            totals[pl.ds(at + g * ROWS, ROWS), :] = jnp.broadcast_to(
                jnp.sum(row_total, axis=1, keepdims=True), (ROWS, HD)
            )

    def mix(i):
        product = jnp.dot(
            weights[block_rows(i), :], v_all[...], preferred_element_type=jnp.float32
        )
        mixed[block_rows(i), :] = (product / totals[block_rows(i), :]).astype(jnp.bfloat16)

    def mixed_to(device):
        return remote(
            mixed.at[rows(device)],
            attended.at[:, lanes(me)],
            o_s,
            o_r,
            {"sp": device},
        )

    def own_mixed():
        return pltpu.make_async_copy(mixed.at[rows(me)], attended.at[:, lanes(me)], o_r)

    def give_back(i):
        for c in range(2):
            device = 2 * chip_of(i) + c

            @pl.when(device == me)
            def _():
                own_mixed().start()

            @pl.when(device != me)
            def _():
                mixed_to(device).start()

    wait_queries(0)
    scores(0, 0)

    def two_blocks(t):
        i = 2 * t
        each(MORE, lambda n: send_more(MORE * i + n))
        wait_queries(i + 1)
        scores(i + 1, 1)
        weigh(i, 0)
        each(MORE, lambda n: send_more(MORE * i + MORE + n))
        wait_queries(i + 2)
        scores(i + 2, 0)
        weigh(i + 1, 1)
        pl.when(t == 1)(change_cores)

    each(chips // 2 - 1, two_blocks)
    make_slopes()
    spread_slopes()
    wait_queries(chips - 1)
    scores(chips - 1, 1)
    weigh(chips - 2, 0)
    weigh(chips - 1, 1)

    def mix_block(i):
        mix(i)
        give_back(i)

    drain(v_all, v_r)
    each(chips + 1, lambda n: mix_block(lax.rem(n, chips)), 1)

    drain(slopes_all.at[pl.ds(0, (chips - 1) * tok)], sl_r)
    each(chips, lambda i: slopes_to(same_core(i), partner, pass_s, pass_r).start(), 1)

    out_tiles = out_cols // HD

    def y_peer(i):
        return lax.rem(y + i, ny)

    class Replicas:
        def __init__(self, bufs, sems):
            self.pack, self.z_in, self.y_out, self.y_in, self.z_out, self.whole = bufs
            self.zi_s, self.zi_r, self.y_s, self.y_r, self.zo_s, self.zo_r = sems

        def z_copy(self, p, origin):
            return remote(
                self.pack.at[p],
                self.z_in.at[origin],
                self.zi_s,
                self.zi_r,
                {"rep": p * ny + y},
            )

        def y_copy(self, p, origin):
            return remote(
                self.y_out,
                self.y_in.at[origin],
                self.y_s,
                self.y_r,
                {"rep": z * ny + p},
            )

        def back_copy(self, p, origin):
            return remote(
                self.z_out,
                self.whole.at[origin],
                self.zo_s,
                self.zo_r,
                {"rep": p * ny + y},
            )

        def start(self):
            each(nz, lambda i: self.z_copy(z_peer(i), z).start(), 1)
            self.z_in[z] = self.pack[z]

        def across(self, more=None):
            drain(self.z_in.at[pl.ds(0, nz - 1)], self.zi_r)
            total = self.z_in[0]
            for p in range(1, nz):
                total = total + self.z_in[p]
            if more is not None:
                total = jnp.concatenate([total, more], axis=0)
            self.y_out[...] = total
            each(ny, lambda i: self.y_copy(y_peer(i), y).start(), 1)
            self.y_in[y] = total

        def back(self):
            drain(self.y_in.at[pl.ds(0, ny - 1)], self.y_r)
            total = self.y_in[0]
            for p in range(1, ny):
                total = total + self.y_in[p]
            self.z_out[...] = total
            each(nz, lambda i: self.back_copy(z_peer(i), z).start(), 1)
            self.whole[z] = total

        def arrive(self):
            drain(self.whole.at[pl.ds(0, nz - 1)], self.zo_r)

        def sent(self):
            drain(self.pack.at[pl.ds(0, nz - 1)], self.zi_s)
            drain(self.y_in.at[pl.ds(0, ny - 1)], self.y_s)
            drain(self.whole.at[pl.ds(0, nz - 1)], self.zo_s)

    drain(slopes_all.at[pl.ds(0, chips * tok)], pass_r)
    grad_in = lax.dot_general(
        mixed[...], slopes_all[...], (((0,), (0,)), ((), ())), preferred_element_type=jnp.float32
    ) * inner ** (-0.5)
    sum_in = Replicas(in_bufs, in_sems)
    sum_out = Replicas(out_bufs, out_sems)
    for p in range(nz):
        sum_in.pack[p] = grad_in[p * in_rows : (p + 1) * in_rows]
    sum_in.start()

    drain(attended, o_r)
    adapted = jnp.dot(
        attended[...], ain_all[...].reshape(inner, rank), preferred_element_type=jnp.float32
    )
    adapted_all[core] = jnp.where(live, adapted * inner ** (-0.5), 0.0).astype(jnp.bfloat16)
    send_adapted = remote(adapted_all.at[core], adapted_all.at[core], ad_s, ad_r, {"sp": partner})
    send_adapted.start()
    send_og.wait_recv()
    send_adapted.wait_recv()
    term_out = lax.dot_general(
        adapted_all[...].reshape(block, rank),
        og_all[...].reshape(block, og_all.shape[2]),
        (((0,), (0,)), ((), ())),
        preferred_element_type=jnp.float32,
    ) * rank ** (-0.5)
    depth = rank // groups

    chip_tiles = out_tiles - 1
    chip_cols = chip_tiles * HD * nz
    for j in range(chips):
        at = 2 * j * depth
        own = jnp.where(
            core == 0, term_out[at : at + depth], term_out[at + depth : at + 2 * depth]
        )
        summed[j] = own[:, :chip_cols]
        for p in range(nz):
            z_first[p, j] = own[:, chip_cols + p * HD : chip_cols + (p + 1) * HD]

    def chunk_to(j, origin):
        return remote(
            summed.at[j],
            chip_in.at[origin],
            chip_s,
            chip_r,
            {"sp": 2 * j + core},
        )

    def z_first_to(p, origin):
        return remote(
            z_first.at[p],
            z_first_in.at[origin],
            zf_s,
            zf_r,
            {"rep": p * ny + y},
        )

    def tile_to(j, origin):
        return remote(
            tiles.at[j], tile_in.at[origin], ti_s, ti_r, {"sp": 2 * j + core}
        )

    each(chips, lambda i: chunk_to(chip_of(i), chip).start(), 1)
    each(nz, lambda i: z_first_to(z_peer(i), z).start(), 1)
    chip_in[chip] = summed[chip]
    z_first_in[z] = z_first[z]

    sum_in.across()
    drain(z_first_in.at[pl.ds(0, nz - 1)], zf_r)
    own = z_first_in[0]
    for p in range(1, nz):
        own = own + z_first_in[p]
    tiles[...] = own
    each(chips, lambda i: tile_to(chip_of(i), chip).start(), 1)
    tile_in[chip] = tiles[chip]

    drain(chip_in.at[pl.ds(0, chips - 1)], chip_r)
    own = chip_in[0]
    for j in range(1, chips):
        own = own + chip_in[j]
    for p in range(nz):
        for t in range(chip_tiles):
            at = (p * chip_tiles + t) * HD
            sum_out.pack[p, t * depth : (t + 1) * depth] = own[:, at : at + HD]
    sum_out.start()
    sum_in.back()
    drain(tile_in.at[pl.ds(0, chips - 1)], ti_r)
    own = tile_in[0]
    for j in range(1, chips):
        own = own + tile_in[j]
    sum_out.across(own)
    sum_in.arrive()
    for p in range(nz):
        gin_ref[p * in_rows : (p + 1) * in_rows] = sum_in.whole[p]
    sum_out.back()

    @pl.when(core != side)
    def _():
        drain(aout_all.at[pl.ds(0, chips), :, z_cols], ao_s)
        drain(ain_all.at[pl.ds(0, chips), z_rows], ai_s)

    @pl.when(core == side)
    def _():
        drain(aout_all.at[pl.ds(0, chips - 1), :, z_cols], ao_s)
        drain(ain_all.at[pl.ds(0, chips - 1), z_rows], ai_s)

    drain(q_all.at[pl.ds(0, tokens - tok), pl.ds(0, HD)], q_s)
    drain(mixed.at[pl.ds(0, tokens - tok)], o_s)
    drain(v_all.at[pl.ds(0, tokens - tok)], v_s)
    drain(others, az_s)
    drain(other_lines, cz_s)
    drain(slopes_all.at[pl.ds(0, chips * tok)], sl_s)
    drain(slopes_all.at[pl.ds(0, (chips - 1) * tok)], pass_s)
    drain(chip_in.at[pl.ds(0, chips - 1)], chip_s)
    drain(tile_in.at[pl.ds(0, chips - 1)], ti_s)
    drain(z_first_in.at[pl.ds(0, nz - 1)], zf_s)
    send_og.wait_send()
    send_adapted.wait_send()
    swap_out.wait_send()
    swap_in.wait_send()
    sum_in.sent()
    sum_out.sent()
    sum_out.arrive()
    for p in range(nz):
        for t in range(chip_tiles):
            at = (p * chip_tiles + t) * HD
            gout_ref[:, at : at + HD] = sum_out.whole[p, t * depth : (t + 1) * depth]
        at = chip_cols + p * HD
        gout_ref[:, at : at + HD] = sum_out.whole[p, chip_tiles * depth :]


def adamw_kernel(*refs):
    ins, outs = refs[:8], refs[8:]
    for at in range(2):
        param, grad, moment, square = (r[...] for r in ins[4 * at : 4 * at + 4])
        for ref, value in zip(outs[3 * at : 3 * at + 3], adamw(param, grad, moment, square)):
            ref[...] = value


def per_device(
    queries,
    key_rows,
    values,
    out_grad,
    clip_count,
    clip_lengths,
    adapter_in,
    adapter_out,
    moment_in,
    square_in,
    moment_out,
    square_out,
):
    tok = queries.shape[1]
    width = out_grad.shape[2]
    rank = adapter_in.shape[1]
    groups = lax.axis_size("sp")
    chips = groups // 2
    reps = lax.axis_size("rep")
    ny = 4 if reps % 4 == 0 and reps > 4 else 1
    nz = reps // ny
    tokens = tok * groups
    depth = rank // groups
    in_lines, out_lines = HD // nz, (width // nz // HD) * depth
    bf16, f32 = jnp.bfloat16, jnp.float32
    vmem = pl.BlockSpec(memory_space=pltpu.VMEM)
    smem = pl.BlockSpec(memory_space=pltpu.SMEM)
    hbm = pl.BlockSpec(memory_space=pl.ANY)
    dma = pltpu.SemaphoreType.DMA

    def sum_bufs(first, lines):
        return [
            pltpu.VMEM((nz, first, HD), f32),
            pltpu.VMEM((nz, first, HD), f32),
            pltpu.VMEM((lines, HD), f32),
            pltpu.VMEM((ny, lines, HD), f32),
            pltpu.VMEM((lines, HD), f32),
            pltpu.VMEM((nz, lines, HD), f32),
        ]

    sum_sems = [dma(())] * 6
    grad_in, grad_out = pl.pallas_call(
        functools.partial(step_kernel, (tok, groups, nz, ny)),
        name="adapter_step",
        out_shape=(
            jax.ShapeDtypeStruct((HD, rank), f32),
            jax.ShapeDtypeStruct((depth, width), f32),
        ),
        in_specs=[smem, smem, hbm, hbm, hbm, hbm, hbm, hbm],
        out_specs=(vmem, vmem),
        scratch_shapes=[
            pltpu.VMEM((tokens, 2 * HD), bf16),
            pltpu.VMEM((tokens, 2 * HD), bf16),
            pltpu.VMEM((tokens, HD), bf16),
            pltpu.VMEM((2, 2 * tok, tokens), f32),
            pltpu.VMEM((2, 2 * tok, HD), f32),
            pltpu.VMEM((tokens, tokens), bf16),
            pltpu.VMEM((tokens, HD), f32),
            pltpu.VMEM((tokens, HD), bf16),
            pltpu.VMEM((tok, groups * HD), bf16),
            pltpu.VMEM((2, tok, width), bf16),
            pltpu.VMEM((HD, rank), f32),
            pltpu.VMEM((depth, width), f32),
            pltpu.VMEM((HD, rank), bf16),
            pltpu.VMEM((depth, width), bf16),
            pltpu.VMEM((groups, HD, rank), bf16),
            pltpu.VMEM((groups, depth, width), bf16),
            pltpu.VMEM((tokens, rank), bf16),
            pltpu.VMEM((2, tok, rank), bf16),
            pltpu.VMEM((chips, depth, width - nz * HD), f32),
            pltpu.VMEM((chips, depth, width - nz * HD), f32),
            pltpu.VMEM((nz, chips, depth, HD), f32),
            pltpu.VMEM((nz, chips, depth, HD), f32),
            pltpu.VMEM((chips, depth, HD), f32),
            pltpu.VMEM((chips, depth, HD), f32),
            sum_bufs(in_lines, in_lines),
            sum_bufs(out_lines - depth, out_lines),
            dma((3,)),
        ]
        + [dma(())] * 9
        + [dma((chips,))]
        + [dma(())] * 20
        + [dma((2,))] * 2
        + [sum_sems, sum_sems],
        compiler_params=pltpu.CompilerParams(
            collective_id=0, has_side_effects=True, vmem_limit_bytes=60 * 2**20
        ),
    )(
        clip_count,
        clip_lengths,
        queries,
        key_rows,
        values,
        out_grad,
        adapter_in,
        adapter_out,
    )
    return tuple(
        pl.pallas_call(
            adamw_kernel,
            name="adamw",
            out_shape=[jax.ShapeDtypeStruct(a.shape, f32) for a in [grad_in] * 3 + [grad_out] * 3],
            in_specs=[vmem] * 8,
            out_specs=[vmem] * 6,
        )(
            adapter_in,
            grad_in,
            moment_in,
            square_in,
            adapter_out,
            grad_out,
            moment_out,
            square_out,
        )
    )


def solution(mesh):
    placed = (
        P("rep", "sp", None),
        P("rep", "sp", None),
        P("rep", "sp", None),
        P("rep", "sp", None),
        P("rep"),
        P("rep", None),
        P("sp", None),
        P("sp", None),
        P("sp", None),
        P("sp", None),
        P("sp", None),
        P("sp", None),
    )
    return jax.shard_map(
        per_device,
        mesh=mesh,
        in_specs=placed,
        out_specs=(
            P("sp", None),
            P("sp", None),
            P("sp", None),
            P("sp", None),
            P("sp", None),
            P("sp", None),
        ),
        check_vma=False,
    )
```

```python
import functools
import math

import jax
import jax.numpy as jnp
from jax import lax
from jax.experimental import pallas as pl
from jax.experimental.pallas import tpu as pltpu
from jax.sharding import PartitionSpec as P

HD = 128
MAX_CLIPS = 3
MESH = pl.DeviceIdType.MESH

first_rate = 0.9
second_rate = 0.999
adam_steps = 100.0
adam_epsilon = 1e-08
decay_rate = 0.1

EXP2_SCALE = HD ** (-0.5) * math.log2(math.e)
MASK = -131072.0
KEY_CHUNKS = 4
EARLY_CHIPS = 6
MORE = 4
ROWS = 64


def adamw(param, grad, moment, square):
    momentum = first_rate * moment + (1.0 - first_rate) * grad
    variance = second_rate * square + (1.0 - second_rate) * grad * grad
    first_hat = momentum / (1.0 - first_rate**adam_steps)
    second_hat = variance / (1.0 - second_rate**adam_steps)
    update = first_hat / (jnp.sqrt(second_hat) + adam_epsilon) + decay_rate * param
    return (momentum, variance, update)


def remote(src, dst, send_sem, recv_sem, device):
    return pltpu.make_async_remote_copy(
        src_ref=src,
        dst_ref=dst,
        send_sem=send_sem,
        recv_sem=recv_sem,
        device_id=device,
        device_id_type=MESH,
    )


def drain(ref, sem):
    pltpu.make_async_copy(ref, ref, sem).wait()


def each(n, body, start=0):
    def step(i, carry):
        body(i)
        return carry

    lax.fori_loop(start, n, step, 0)


def step_kernel(
    dims,
    count_ref,
    lengths_ref,
    q_hbm,
    k_hbm,
    v_hbm,
    og_hbm,
    ain_hbm,
    aout_hbm,
    gin_ref,
    gout_ref,
    q_all,
    k_all,
    v_all,
    scores_buf,
    high_buf,
    weights,
    totals,
    mixed,
    attended,
    og_all,
    ain_own,
    aout_own,
    ain_cast,
    aout_cast,
    ain_all,
    aout_all,
    slopes_all,
    adapted_all,
    summed,
    chip_in,
    z_first,
    z_first_in,
    tiles,
    tile_in,
    in_bufs,
    out_bufs,
    load_sems,
    og_s,
    og_r,
    ad_s,
    ad_r,
    k_s,
    k_r,
    v_s,
    v_r,
    q_s,
    q_r,
    o_s,
    o_r,
    ai_s,
    ai_r,
    ao_s,
    ao_r,
    sl_s,
    sl_r,
    pass_s,
    pass_r,
    chip_s,
    chip_r,
    ti_s,
    ti_r,
    zf_s,
    zf_r,
    az_s,
    az_r,
    cz_s,
    cz_r,
    half_s,
    half_r,
    in_sems,
    out_sems,
):
    tok, groups, nz, ny = dims
    chips = groups // 2
    tokens = tok * groups
    rank = ain_hbm.shape[1]
    inner = HD * groups
    me = lax.axis_index("sp")
    rep = lax.axis_index("rep")
    chip = me // 2
    core = lax.rem(me, 2)
    partner = me + 1 - 2 * core
    z = rep // ny
    y = lax.rem(rep, ny)

    def rows(s):
        return pl.ds(pl.multiple_of(s * tok, tok), tok)

    def lanes(s):
        return pl.ds(pl.multiple_of(s * HD, HD), HD)

    def same_core(i):
        return 2 * lax.rem(chip + i, chips) + core

    barrier = pltpu.get_barrier_semaphore()

    def greet_sp(i):
        pl.semaphore_signal(
            barrier, inc=1, device_id={"sp": lax.rem(me + i, groups)}, device_id_type=MESH
        )

    def greet_z(i):
        pl.semaphore_signal(
            barrier,
            inc=1,
            device_id={"rep": lax.rem(z + i, nz) * ny + y},
            device_id_type=MESH,
        )

    def greet_y(i):
        pl.semaphore_signal(
            barrier,
            inc=1,
            device_id={"rep": z * ny + lax.rem(y + i, ny)},
            device_id_type=MESH,
        )

    each(groups, greet_sp, 1)
    each(nz, greet_z, 1)
    each(ny, greet_y, 1)

    load_og = pltpu.make_async_copy(og_hbm.at[0], og_all.at[core], load_sems.at[0])
    load_ain = pltpu.make_async_copy(ain_hbm, ain_own, load_sems.at[1])
    load_aout = pltpu.make_async_copy(aout_hbm, aout_own, load_sems.at[2])
    load_ain.start()
    load_aout.start()
    load_og.start()
    pl.semaphore_wait(barrier, groups + nz + ny - 3)

    def head_to(src, dst, s, r, device):
        return remote(
            src.at[0, :, lanes(device)],
            dst.at[rows(me), pl.ds(0, HD)],
            s,
            r,
            {"sp": device},
        )

    def own_head(src, dst, r):
        return pltpu.make_async_copy(
            src.at[0, :, lanes(me)], dst.at[rows(me), pl.ds(0, HD)], r
        )

    def to_peer(i):
        return lax.rem(me - i + groups, groups)


    half = groups // 2
    in_rows = HD // nz
    out_cols = gout_ref.shape[1] // nz
    side = me // half
    z_cols = pl.ds(pl.multiple_of(z * out_cols, out_cols), out_cols)
    z_rows = pl.ds(pl.multiple_of(z * in_rows, in_rows), in_rows)

    def share_device(i):
        return 2 * lax.rem(chip + i, chips) + side

    def aout_share(device):
        return remote(
            aout_cast.at[:, z_cols],
            aout_all.at[me, :, z_cols],
            ao_s,
            ao_r,
            {"sp": device},
        )

    def ain_share(device):
        return remote(
            ain_cast.at[z_rows], ain_all.at[me, z_rows], ai_s, ai_r, {"sp": device}
        )

    load_ain.wait()
    load_aout.wait()
    ain_cast[...] = ain_own[...].astype(jnp.bfloat16)
    aout_cast[...] = aout_own[...].astype(jnp.bfloat16)

    @pl.when(core == side)
    def _():
        pltpu.make_async_copy(
            aout_cast.at[:, z_cols], aout_all.at[me, :, z_cols], ao_r
        ).start()
        pltpu.make_async_copy(ain_cast.at[z_rows], ain_all.at[me, z_rows], ai_r).start()

    @pl.when(core != side)
    def _():
        aout_share(partner).start()
        ain_share(partner).start()

    def send_share(i):
        aout_share(share_device(i)).start()
        ain_share(share_device(i)).start()

    each(chips, send_share, 1)

    def to_chip(src, dst, send, recv, j):
        for c in range(2):
            head_to(src, dst, send, recv, 2 * lax.rem(chip - j + chips, chips) + c).start()

    def queries_to(j):
        to_chip(q_hbm, q_all, q_s, q_r.at[chip], j)

    def values_to(j):
        to_chip(v_hbm, v_all, v_s, v_r, j)

    own_head(k_hbm, k_all, k_r).start()
    each(groups, lambda i: head_to(k_hbm, k_all, k_s, k_r, to_peer(i)).start(), 1)
    own_head(q_hbm, q_all, q_r.at[chip]).start()
    own_head(v_hbm, v_all, v_r).start()
    head_to(q_hbm, q_all, q_s, q_r.at[chip], partner).start()
    head_to(v_hbm, v_all, v_s, v_r, partner).start()
    queries_to(1)

    send_og = remote(og_hbm.at[0], og_all.at[core], og_s, og_r, {"sp": partner})
    send_og.start()

    ends = []
    for j in range(MAX_CLIPS):
        length = jnp.where(count_ref[0] > j, lengths_ref[0, j], 0)
        ends.append(length if j == 0 else ends[-1] + length)

    def segment(positions):
        return sum((positions >= e).astype(jnp.int32) for e in ends)

    block = 2 * tok

    def features(b):
        r = pl.ds(pl.multiple_of(b * block, block), block)
        at = b * block + lax.broadcasted_iota(jnp.int32, (block, HD), 0)
        feature = lax.broadcasted_iota(jnp.int32, (block, HD), 1)
        seg = segment(at)
        same = seg == feature
        k_all[r, HD:] = jnp.where(same, 1.0, 0.0).astype(jnp.bfloat16)
        other = jnp.where(feature <= MAX_CLIPS, MASK, 0.0)
        q_all[r, HD:] = jnp.where(same, 0.0, other).astype(jnp.bfloat16)

    each(chips, features)
    mine = me * tok + lax.broadcasted_iota(jnp.int32, (tok, rank), 0)
    live = segment(mine) < MAX_CLIPS

    owners = pl.ds(pl.multiple_of(core * half, half), half)

    drain(aout_all.at[owners, :, z_cols], ao_r)
    drain(ain_all.at[owners, z_rows], ai_r)

    def z_peer(i):
        return lax.rem(z + i, nz)

    def aout_along(p, origin):
        cols = pl.ds(pl.multiple_of(origin * out_cols, out_cols), out_cols)
        part = aout_all.at[owners, :, cols]
        return remote(part, part, az_s, az_r, {"rep": p * ny + y})

    def ain_along(p, origin):
        lines = pl.ds(pl.multiple_of(origin * in_rows, in_rows), in_rows)
        part = ain_all.at[owners, lines]
        return remote(part, part, cz_s, cz_r, {"rep": p * ny + y})

    def send_along(i):
        aout_along(z_peer(i), z).start()
        ain_along(z_peer(i), z).start()

    each(nz, send_along, 1)

    others = aout_all.at[owners, :, pl.ds(0, (nz - 1) * out_cols)]
    other_lines = ain_all.at[owners, pl.ds(0, (nz - 1) * in_rows)]

    swap_out = remote(
        aout_all.at[owners], aout_all.at[owners], half_s.at[0], half_r.at[0], {"sp": partner}
    )
    swap_in = remote(
        ain_all.at[owners], ain_all.at[owners], half_s.at[1], half_r.at[1], {"sp": partner}
    )

    def slopes_to(owner, device, s, r):
        part = slopes_all.at[rows(owner)]
        return remote(part, part, s, r, {"sp": device})

    def change_cores():
        drain(others, az_r)
        drain(other_lines, cz_r)
        swap_out.start()
        swap_in.start()

    def make_slopes():
        swap_out.wait_recv()
        swap_in.wait_recv()
        load_og.wait()
        outer = jnp.concatenate([aout_all[i].astype(jnp.float32) for i in range(groups)], axis=0)
        slopes = lax.dot_general(
            og_all[core],
            outer.astype(jnp.bfloat16),
            (((1,), (1,)), ((), ())),
            preferred_element_type=jnp.float32,
        ) * rank ** (-0.5)
        slopes_all[rows(me)] = jnp.where(live, slopes, 0.0).astype(jnp.bfloat16)

    def spread_slopes():
        slopes_to(me, partner, sl_s, pass_r).start()
        each(chips, lambda i: slopes_to(me, same_core(i), sl_s, sl_r).start(), 1)

    drain(k_all.at[pl.ds(0, tokens - tok), pl.ds(0, HD)], k_s)
    each(EARLY_CHIPS, queries_to, 2)

    def send_more(n):
        pl.when(n < chips - EARLY_CHIPS)(lambda: queries_to(EARLY_CHIPS + n))
        j = n - (chips - EARLY_CHIPS) + 1
        pl.when((j >= 1) & (j < chips))(lambda: values_to(j))

    drain(k_all.at[:, pl.ds(0, HD)], k_r)

    def chip_of(i):
        return lax.rem(chip + i, chips)

    def block_rows(i):
        return pl.ds(pl.multiple_of(chip_of(i) * block, block), block)

    def wait_queries(i):
        drain(q_all.at[block_rows(i), pl.ds(0, HD)], q_r.at[chip_of(i)])

    width = tokens // KEY_CHUNKS

    def scores(i, slot):
        query = q_all[block_rows(i), :]
        high = None
        for c in range(KEY_CHUNKS):
            s = lax.dot_general(
                query,
                k_all[c * width : (c + 1) * width, :],
                (((1,), (1,)), ((), ())),
                preferred_element_type=jnp.float32,
            )
            scores_buf[slot, :, c * width : (c + 1) * width] = s
            for j in range(width // HD):
                piece = s[:, j * HD : (j + 1) * HD]
                high = piece if high is None else jnp.maximum(high, piece)
        high_buf[slot] = jnp.broadcast_to(jnp.max(high, axis=1, keepdims=True), (block, HD))

    def weigh(i, slot):
        at = pl.multiple_of(chip_of(i) * block, block)
        for g in range(block // ROWS):
            lines = slice(g * ROWS, (g + 1) * ROWS)
            high = high_buf[slot, lines]
            row_total = None
            for j in range(tokens // HD):
                s = scores_buf[slot, lines, j * HD : (j + 1) * HD]
                exponent = jnp.exp2((s - high) * EXP2_SCALE)
                row_total = exponent if row_total is None else row_total + exponent
                weights[pl.ds(at + g * ROWS, ROWS), j * HD : (j + 1) * HD] = exponent.astype(
                    jnp.bfloat16
                )
            totals[pl.ds(at + g * ROWS, ROWS), :] = jnp.broadcast_to(
                jnp.sum(row_total, axis=1, keepdims=True), (ROWS, HD)
            )

    def mix(i):
        product = jnp.dot(
            weights[block_rows(i), :], v_all[...], preferred_element_type=jnp.float32
        )
        mixed[block_rows(i), :] = (product / totals[block_rows(i), :]).astype(jnp.bfloat16)

    def mixed_to(device):
        return remote(
            mixed.at[rows(device)],
            attended.at[:, lanes(me)],
            o_s,
            o_r,
            {"sp": device},
        )

    def own_mixed():
        return pltpu.make_async_copy(mixed.at[rows(me)], attended.at[:, lanes(me)], o_r)

    def give_back(i):
        for c in range(2):
            device = 2 * chip_of(i) + c

            @pl.when(device == me)
            def _():
                own_mixed().start()

            @pl.when(device != me)
            def _():
                mixed_to(device).start()

    wait_queries(0)
    scores(0, 0)

    def two_blocks(t):
        i = 2 * t
        each(MORE, lambda n: send_more(MORE * i + n))
        wait_queries(i + 1)
        scores(i + 1, 1)
        weigh(i, 0)
        each(MORE, lambda n: send_more(MORE * i + MORE + n))
        wait_queries(i + 2)
        scores(i + 2, 0)
        weigh(i + 1, 1)
        pl.when(t == 1)(change_cores)

    each(chips // 2 - 1, two_blocks)
    make_slopes()
    wait_queries(chips - 1)
    scores(chips - 1, 1)
    weigh(chips - 2, 0)
    weigh(chips - 1, 1)

    drain(v_all.at[pl.ds(0, tokens - tok)], v_s)
    spread_slopes()

    def mix_block(i):
        mix(i)
        give_back(i)

    drain(v_all, v_r)
    each(chips + 1, lambda n: mix_block(lax.rem(n, chips)), 1)

    drain(slopes_all.at[pl.ds(0, (chips - 1) * tok)], sl_r)
    each(chips, lambda i: slopes_to(same_core(i), partner, pass_s, pass_r).start(), 1)

    out_tiles = out_cols // HD

    def y_peer(i):
        return lax.rem(y + i, ny)

    class Replicas:
        def __init__(self, bufs, sems):
            self.pack, self.z_in, self.y_out, self.y_in, self.z_out, self.whole = bufs
            self.zi_s, self.zi_r, self.y_s, self.y_r, self.zo_s, self.zo_r = sems

        def z_copy(self, p, origin):
            return remote(
                self.pack.at[p],
                self.z_in.at[origin],
                self.zi_s,
                self.zi_r,
                {"rep": p * ny + y},
            )

        def y_copy(self, p, origin):
            return remote(
                self.y_out,
                self.y_in.at[origin],
                self.y_s,
                self.y_r,
                {"rep": z * ny + p},
            )

        def back_copy(self, p, origin):
            return remote(
                self.z_out,
                self.whole.at[origin],
                self.zo_s,
                self.zo_r,
                {"rep": p * ny + y},
            )

        def start(self):
            each(nz, lambda i: self.z_copy(z_peer(i), z).start(), 1)
            self.z_in[z] = self.pack[z]

        def across(self, more=None):
            drain(self.z_in.at[pl.ds(0, nz - 1)], self.zi_r)
            total = self.z_in[0]
            for p in range(1, nz):
                total = total + self.z_in[p]
            if more is not None:
                total = jnp.concatenate([total, more], axis=0)
            self.y_out[...] = total
            each(ny, lambda i: self.y_copy(y_peer(i), y).start(), 1)
            self.y_in[y] = total

        def back(self):
            drain(self.y_in.at[pl.ds(0, ny - 1)], self.y_r)
            total = self.y_in[0]
            for p in range(1, ny):
                total = total + self.y_in[p]
            self.z_out[...] = total
            each(nz, lambda i: self.back_copy(z_peer(i), z).start(), 1)
            self.whole[z] = total

        def arrive(self):
            drain(self.whole.at[pl.ds(0, nz - 1)], self.zo_r)

        def sent(self):
            drain(self.pack.at[pl.ds(0, nz - 1)], self.zi_s)
            drain(self.y_in.at[pl.ds(0, ny - 1)], self.y_s)
            drain(self.whole.at[pl.ds(0, nz - 1)], self.zo_s)

    drain(slopes_all.at[pl.ds(0, chips * tok)], pass_r)
    grad_in = lax.dot_general(
        mixed[...], slopes_all[...], (((0,), (0,)), ((), ())), preferred_element_type=jnp.float32
    ) * inner ** (-0.5)
    sum_in = Replicas(in_bufs, in_sems)
    sum_out = Replicas(out_bufs, out_sems)
    for p in range(nz):
        sum_in.pack[p] = grad_in[p * in_rows : (p + 1) * in_rows]
    sum_in.start()

    drain(attended, o_r)
    adapted = jnp.dot(
        attended[...], ain_all[...].reshape(inner, rank), preferred_element_type=jnp.float32
    )
    adapted_all[core] = jnp.where(live, adapted * inner ** (-0.5), 0.0).astype(jnp.bfloat16)
    send_adapted = remote(adapted_all.at[core], adapted_all.at[core], ad_s, ad_r, {"sp": partner})
    send_adapted.start()
    send_og.wait_recv()
    send_adapted.wait_recv()
    term_out = lax.dot_general(
        adapted_all[...].reshape(block, rank),
        og_all[...].reshape(block, og_all.shape[2]),
        (((0,), (0,)), ((), ())),
        preferred_element_type=jnp.float32,
    ) * rank ** (-0.5)
    depth = rank // groups

    chip_tiles = out_tiles - 1
    chip_cols = chip_tiles * HD * nz
    for j in range(chips):
        at = 2 * j * depth
        own = jnp.where(
            core == 0, term_out[at : at + depth], term_out[at + depth : at + 2 * depth]
        )
        summed[j] = own[:, :chip_cols]
        for p in range(nz):
            z_first[p, j] = own[:, chip_cols + p * HD : chip_cols + (p + 1) * HD]

    def chunk_to(j, origin):
        return remote(
            summed.at[j],
            chip_in.at[origin],
            chip_s,
            chip_r,
            {"sp": 2 * j + core},
        )

    def z_first_to(p, origin):
        return remote(
            z_first.at[p],
            z_first_in.at[origin],
            zf_s,
            zf_r,
            {"rep": p * ny + y},
        )

    def tile_to(j, origin):
        return remote(
            tiles.at[j], tile_in.at[origin], ti_s, ti_r, {"sp": 2 * j + core}
        )

    each(chips, lambda i: chunk_to(chip_of(i), chip).start(), 1)
    each(nz, lambda i: z_first_to(z_peer(i), z).start(), 1)
    chip_in[chip] = summed[chip]
    z_first_in[z] = z_first[z]

    sum_in.across()
    drain(z_first_in.at[pl.ds(0, nz - 1)], zf_r)
    own = z_first_in[0]
    for p in range(1, nz):
        own = own + z_first_in[p]
    tiles[...] = own
    each(chips, lambda i: tile_to(chip_of(i), chip).start(), 1)
    tile_in[chip] = tiles[chip]

    drain(chip_in.at[pl.ds(0, chips - 1)], chip_r)
    own = chip_in[0]
    for j in range(1, chips):
        own = own + chip_in[j]
    for p in range(nz):
        for t in range(chip_tiles):
            at = (p * chip_tiles + t) * HD
            sum_out.pack[p, t * depth : (t + 1) * depth] = own[:, at : at + HD]
    sum_out.start()
    sum_in.back()
    drain(tile_in.at[pl.ds(0, chips - 1)], ti_r)
    own = tile_in[0]
    for j in range(1, chips):
        own = own + tile_in[j]
    sum_out.across(own)
    sum_in.arrive()
    for p in range(nz):
        gin_ref[p * in_rows : (p + 1) * in_rows] = sum_in.whole[p]
    sum_out.back()

    @pl.when(core != side)
    def _():
        drain(aout_all.at[pl.ds(0, chips), :, z_cols], ao_s)
        drain(ain_all.at[pl.ds(0, chips), z_rows], ai_s)

    @pl.when(core == side)
    def _():
        drain(aout_all.at[pl.ds(0, chips - 1), :, z_cols], ao_s)
        drain(ain_all.at[pl.ds(0, chips - 1), z_rows], ai_s)

    drain(q_all.at[pl.ds(0, tokens - tok), pl.ds(0, HD)], q_s)
    drain(mixed.at[pl.ds(0, tokens - tok)], o_s)
    drain(others, az_s)
    drain(other_lines, cz_s)
    drain(slopes_all.at[pl.ds(0, chips * tok)], sl_s)
    drain(slopes_all.at[pl.ds(0, (chips - 1) * tok)], pass_s)
    drain(chip_in.at[pl.ds(0, chips - 1)], chip_s)
    drain(tile_in.at[pl.ds(0, chips - 1)], ti_s)
    drain(z_first_in.at[pl.ds(0, nz - 1)], zf_s)
    send_og.wait_send()
    send_adapted.wait_send()
    swap_out.wait_send()
    swap_in.wait_send()
    sum_in.sent()
    sum_out.sent()
    sum_out.arrive()
    for p in range(nz):
        for t in range(chip_tiles):
            at = (p * chip_tiles + t) * HD
            gout_ref[:, at : at + HD] = sum_out.whole[p, t * depth : (t + 1) * depth]
        at = chip_cols + p * HD
        gout_ref[:, at : at + HD] = sum_out.whole[p, chip_tiles * depth :]


def adamw_kernel(*refs):
    ins, outs = refs[:8], refs[8:]
    for at in range(2):
        param, grad, moment, square = (r[...] for r in ins[4 * at : 4 * at + 4])
        for ref, value in zip(outs[3 * at : 3 * at + 3], adamw(param, grad, moment, square)):
            ref[...] = value


def per_device(
    queries,
    key_rows,
    values,
    out_grad,
    clip_count,
    clip_lengths,
    adapter_in,
    adapter_out,
    moment_in,
    square_in,
    moment_out,
    square_out,
):
    tok = queries.shape[1]
    width = out_grad.shape[2]
    rank = adapter_in.shape[1]
    groups = lax.axis_size("sp")
    chips = groups // 2
    reps = lax.axis_size("rep")
    ny = 4 if reps % 4 == 0 and reps > 4 else 1
    nz = reps // ny
    tokens = tok * groups
    depth = rank // groups
    in_lines, out_lines = HD // nz, (width // nz // HD) * depth
    bf16, f32 = jnp.bfloat16, jnp.float32
    vmem = pl.BlockSpec(memory_space=pltpu.VMEM)
    smem = pl.BlockSpec(memory_space=pltpu.SMEM)
    hbm = pl.BlockSpec(memory_space=pl.ANY)
    dma = pltpu.SemaphoreType.DMA

    def sum_bufs(first, lines):
        return [
            pltpu.VMEM((nz, first, HD), f32),
            pltpu.VMEM((nz, first, HD), f32),
            pltpu.VMEM((lines, HD), f32),
            pltpu.VMEM((ny, lines, HD), f32),
            pltpu.VMEM((lines, HD), f32),
            pltpu.VMEM((nz, lines, HD), f32),
        ]

    sum_sems = [dma(())] * 6
    grad_in, grad_out = pl.pallas_call(
        functools.partial(step_kernel, (tok, groups, nz, ny)),
        name="adapter_step",
        out_shape=(
            jax.ShapeDtypeStruct((HD, rank), f32),
            jax.ShapeDtypeStruct((depth, width), f32),
        ),
        in_specs=[smem, smem, hbm, hbm, hbm, hbm, hbm, hbm],
        out_specs=(vmem, vmem),
        scratch_shapes=[
            pltpu.VMEM((tokens, 2 * HD), bf16),
            pltpu.VMEM((tokens, 2 * HD), bf16),
            pltpu.VMEM((tokens, HD), bf16),
            pltpu.VMEM((2, 2 * tok, tokens), f32),
            pltpu.VMEM((2, 2 * tok, HD), f32),
            pltpu.VMEM((tokens, tokens), bf16),
            pltpu.VMEM((tokens, HD), f32),
            pltpu.VMEM((tokens, HD), bf16),
            pltpu.VMEM((tok, groups * HD), bf16),
            pltpu.VMEM((2, tok, width), bf16),
            pltpu.VMEM((HD, rank), f32),
            pltpu.VMEM((depth, width), f32),
            pltpu.VMEM((HD, rank), bf16),
            pltpu.VMEM((depth, width), bf16),
            pltpu.VMEM((groups, HD, rank), bf16),
            pltpu.VMEM((groups, depth, width), bf16),
            pltpu.VMEM((tokens, rank), bf16),
            pltpu.VMEM((2, tok, rank), bf16),
            pltpu.VMEM((chips, depth, width - nz * HD), f32),
            pltpu.VMEM((chips, depth, width - nz * HD), f32),
            pltpu.VMEM((nz, chips, depth, HD), f32),
            pltpu.VMEM((nz, chips, depth, HD), f32),
            pltpu.VMEM((chips, depth, HD), f32),
            pltpu.VMEM((chips, depth, HD), f32),
            sum_bufs(in_lines, in_lines),
            sum_bufs(out_lines - depth, out_lines),
            dma((3,)),
        ]
        + [dma(())] * 9
        + [dma((chips,))]
        + [dma(())] * 20
        + [dma((2,))] * 2
        + [sum_sems, sum_sems],
        compiler_params=pltpu.CompilerParams(
            collective_id=0, has_side_effects=True, vmem_limit_bytes=60 * 2**20
        ),
    )(
        clip_count,
        clip_lengths,
        queries,
        key_rows,
        values,
        out_grad,
        adapter_in,
        adapter_out,
    )
    return tuple(
        pl.pallas_call(
            adamw_kernel,
            name="adamw",
            out_shape=[jax.ShapeDtypeStruct(a.shape, f32) for a in [grad_in] * 3 + [grad_out] * 3],
            in_specs=[vmem] * 8,
            out_specs=[vmem] * 6,
        )(
            adapter_in,
            grad_in,
            moment_in,
            square_in,
            adapter_out,
            grad_out,
            moment_out,
            square_out,
        )
    )


def solution(mesh):
    placed = (
        P("rep", "sp", None),
        P("rep", "sp", None),
        P("rep", "sp", None),
        P("rep", "sp", None),
        P("rep"),
        P("rep", None),
        P("sp", None),
        P("sp", None),
        P("sp", None),
        P("sp", None),
        P("sp", None),
        P("sp", None),
    )
    return jax.shard_map(
        per_device,
        mesh=mesh,
        in_specs=placed,
        out_specs=(
            P("sp", None),
            P("sp", None),
            P("sp", None),
            P("sp", None),
            P("sp", None),
            P("sp", None),
        ),
        check_vma=False,
    )
```
